128 devices in a mesh: qx: 8 (over y, core), qy: 16 (over x, z).
Axes of the slice: x: 4, y: 4, z: 4, core: 2. Of those that a mesh axis runs over, the one named last changes fastest.
Arguments:
- positions: float32 [32, 64, 2, 256], replicated, may hold values from 0 to 64, as said below
- samples: bfloat16 [32, 64, 256, 256], P('qx', 'qy'), may hold values from -6 to 6
- leaf_basis: bfloat16 [32, 64, 256, 256], P('qx', 'qy'), may hold values from -0.375 to 0.375
- transfer_one: bfloat16 [32, 64, 256, 256], P('qx', 'qy'), may hold values from -0.25 to 0.25
- transfer_two: bfloat16 [16, 32, 256, 256], P('qx', 'qy'), may hold values from -0.25 to 0.25
- couplings: bfloat16 [3, 20, 256, 256], replicated, may hold values from -0.078125 to 0.078125
- near_lists: int32 [32, 64, 9], P('qx', 'qy'), may hold values from -1 to 2047, as said below
- far_zero: int32 [32, 64, 27], P('qx', 'qy'), may hold values from -1 to 2047, as said below
- far_one: int32 [16, 32, 27], P('qx', 'qy'), may hold values from -1 to 511, as said below
- far_two: int32 [8, 16, 27], P('qx', 'qy'), may hold values from -1 to 127, as said below
Outputs:
- product: bfloat16 [32, 64, 256, 256], P('qx', 'qy')
The draws below stay inside these ranges and needn't reach their ends.
Inputs may be any that keep to these rules, and one draw needn't show every extreme that they name: Site p of leaf (i, j) lies at positions[i, j, 0, p] between i and i + 1 and positions[i, j, 1, p] between j and j + 1. `near_lists`: every entry of the list of leaf (i, j) is -1 or the id r * 64 + c of a leaf (r, c) with abs(r - i) <= 1 and abs(c - j) <= 1; the leaf's own id is always in its list, and no id stands twice. `far_zero`: every entry of the list of leaf (i, j) is -1 or the id r * 64 + c of a leaf (r, c) with max(abs(r - i), abs(c - j)) >= 2 whose parent (r // 2, c // 2) is within one step of (i // 2, j // 2) along each coordinate; no id stands twice. `far_one`: every entry of the list of level-1 cell (i, j) is -1 or the id r * 32 + c of a level-1 cell (r, c) with max(abs(r - i), abs(c - j)) >= 2 and (r // 2, c // 2) within one step of (i // 2, j // 2) along each coordinate; no id stands twice. `far_two`: every entry of the list of level-2 cell (i, j) is -1 or the id r * 16 + c of a level-2 cell (r, c) with max(abs(r - i), abs(c - j)) >= 2 and (r // 2, c // 2) within one step of (i // 2, j // 2) along each coordinate; no id stands twice.
All inputs are finite; a program needn't handle non-finite values.
Results may differ from the reference program's by a relative error of at most 0.0085.
Values may be sent and summed in bfloat16 or wider, within the bound.
A program may use at most 256 MiB of HBM per device.

```python
import jax
import jax.numpy as jnp
import numpy as np
from jax import lax

LEAF = 256
RANK = 256
COLS = 256
SIDE = 4
NEAR = 9
FAR = 27
HALF = 20
LEVELS = 3
GX0 = 32
GY0 = 64
GX1 = 16
GY1 = 32
GX2 = 8
GY2 = 16


def crowded_cells(key, grid_rows, grid_cols, cell_leaves):
    centre_row = jax.random.randint(jax.random.fold_in(key, 7), (), 0, GX0)
    centre_col = jax.random.randint(jax.random.fold_in(key, 8), (), 0, GY0)
    mid_rows = jnp.arange(grid_rows, dtype=jnp.int32) * cell_leaves + cell_leaves // 2
    mid_cols = jnp.arange(grid_cols, dtype=jnp.int32) * cell_leaves + cell_leaves // 2
    reach_leaves = 3 * SIDE
    near_rows = jnp.abs(mid_rows - centre_row) <= reach_leaves
    near_cols = jnp.abs(mid_cols - centre_col) <= reach_leaves
    return near_rows[:, None] & near_cols[None, :]


def far_lists(key, grid_rows, grid_cols, cell_leaves, salt):
    crowded = crowded_cells(key, grid_rows, grid_cols, cell_leaves)
    row_ids = jnp.arange(grid_rows, dtype=jnp.int32)[:, None, None]
    col_ids = jnp.arange(grid_cols, dtype=jnp.int32)[None, :, None]
    slot_ids = jnp.arange(36, dtype=jnp.int32)[None, None, :]
    source_row = row_ids + slot_ids // 6 - 2 - row_ids % 2
    source_col = col_ids + slot_ids % 6 - 2 - col_ids % 2
    adjacent = (jnp.abs(source_row - row_ids) <= 1) & (jnp.abs(source_col - col_ids) <= 1)
    inside = (source_row >= 0) & (source_row < grid_rows) & (source_col >= 0) & (source_col < grid_cols)
    coin_flips = jax.random.randint(jax.random.fold_in(key, salt), (grid_rows, grid_cols, 36), 0, 2) == 0
    retained = inside & jnp.logical_not(adjacent) & (crowded[:, :, None] | coin_flips)
    source_ids = jnp.where(retained, source_row * grid_cols + source_col, -1)
    scores = jax.random.randint(jax.random.fold_in(key, salt + 1), (grid_rows, grid_cols, 36), 0, 1 << 20) * 64 + slot_ids
    scores = scores + jnp.where(adjacent, 1 << 27, 0)
    ordering = jnp.argsort(scores, axis=-1)[:, :, :FAR]
    return jnp.take_along_axis(source_ids, ordering, axis=-1).astype(jnp.int32)


def draw_positions(key, part):
    array_shape = (GX0, GY0, 2, LEAF)
    inside_cell = jax.random.uniform(key, array_shape, jnp.float32, 0.005, 0.995)
    row_base = jnp.arange(GX0, dtype=jnp.float32)[:, None, None]
    col_base = jnp.arange(GY0, dtype=jnp.float32)[None, :, None]
    return jnp.stack([inside_cell[:, :, 0] + row_base, inside_cell[:, :, 1] + col_base], axis=2)


def draw_near_lists(key, part):
    crowded = crowded_cells(key, GX0, GY0, 1)
    row_ids = jnp.arange(GX0, dtype=jnp.int32)[:, None, None]
    col_ids = jnp.arange(GY0, dtype=jnp.int32)[None, :, None]
    slot_ids = jnp.arange(NEAR, dtype=jnp.int32)[None, None, :]
    source_row = row_ids + slot_ids // 3 - 1
    source_col = col_ids + slot_ids % 3 - 1
    inside = (source_row >= 0) & (source_row < GX0) & (source_col >= 0) & (source_col < GY0)
    coin_flips = jax.random.randint(jax.random.fold_in(key, 11), (GX0, GY0, NEAR), 0, 3) == 0
    retained = inside & ((slot_ids == 4) | crowded[:, :, None] | coin_flips)
    source_ids = jnp.where(retained, source_row * GY0 + source_col, -1)
    scores = jax.random.randint(jax.random.fold_in(key, 13), (GX0, GY0, NEAR), 0, 1 << 20) * 16 + slot_ids
    ordering = jnp.argsort(scores, axis=-1)
    return jnp.take_along_axis(source_ids, ordering, axis=-1).astype(jnp.int32)


def draw_far_zero(key, part):
    return far_lists(key, GX0, GY0, 1, 21)


def draw_far_one(key, part):
    return far_lists(key, GX1, GY1, 2, 23)


def draw_far_two(key, part):
    return far_lists(key, GX2, GY2, 4, 25)


def block_levels(own_key, shape, shards, low, high):
    gain = 1.0
    for axis_at, blocks in shards:
        heights = jax.random.uniform(jax.random.fold_in(jax.random.fold_in(own_key, 6), axis_at), (blocks,), jnp.float32, low / len(shards), high / len(shards))
        gain = gain * jnp.repeat(jnp.exp(heights), shape[axis_at] // blocks).reshape((-1,) + (1,) * (len(shape) - 1 - axis_at))
    return gain


def gaussian(own_key, extent, scale, reach, split=(), kind=jnp.bfloat16):
    factor_of = block_levels(own_key, extent, split, -0.22, 0.18) if split else 1.0
    values = jax.random.normal(own_key, extent, jnp.float32) * scale * factor_of
    return jnp.minimum(jnp.maximum(values, -reach), reach).astype(kind)


def setup_inputs(seed: int = 0) -> dict:
    splits = jax.random.split(jax.random.key(seed), 11)
    positions = draw_positions(jax.random.fold_in(splits[10], 71), 0)
    samples = gaussian(splits[1], (GX0, GY0, LEAF, COLS), 1.0, 6.0, ((0, 8), (1, 16)))
    leaf_basis = gaussian(splits[2], (GX0, GY0, LEAF, RANK), LEAF ** -0.5, 0.375, ((0, 8), (1, 16)))
    transfer_one = gaussian(splits[3], (GX0, GY0, RANK, RANK), (2 * RANK) ** -0.5, 0.25, ((0, 8), (1, 16)))
    transfer_two = gaussian(splits[4], (GX1, GY1, RANK, RANK), (2 * RANK) ** -0.5, 0.25, ((0, 8), (1, 16)))
    couplings = gaussian(splits[5], (LEVELS, HALF, RANK, RANK), (FAR * RANK) ** -0.5, 0.078125)
    near_lists = draw_near_lists(jax.random.fold_in(splits[10], 71), 0)
    far_zero = draw_far_zero(jax.random.fold_in(splits[10], 71), 0)
    far_one = draw_far_one(jax.random.fold_in(splits[10], 71), 0)
    far_two = draw_far_two(jax.random.fold_in(splits[10], 71), 0)
    return dict(positions=positions, samples=samples, leaf_basis=leaf_basis, transfer_one=transfer_one, transfer_two=transfer_two, couplings=couplings, near_lists=near_lists, far_zero=far_zero, far_one=far_one, far_two=far_two)


root_three = 1.7320508075688772
length_scale = 1.0

def offset_plan():
    slot_of = np.zeros((49,), np.int32)
    flip_of = np.zeros((49,), np.int32)
    active = np.zeros((49,), np.int32)
    upper_half = []
    for number in range(49):
        row_step = number // 7 - 3
        col_step = number % 7 - 3
        if max(abs(row_step), abs(col_step)) >= 2 and (row_step > 0 or (row_step == 0 and col_step > 0)):
            upper_half.append(number)
    for number in range(49):
        row_step = number // 7 - 3
        col_step = number % 7 - 3
        if max(abs(row_step), abs(col_step)) >= 2:
            active[number] = 1
            if number in upper_half:
                slot_of[number] = upper_half.index(number)
            else:
                slot_of[number] = upper_half.index((3 - row_step) * 7 + 3 - col_step)
                flip_of[number] = 1
    return (slot_of, flip_of, active)

def coupling_table(level_couplings):
    slot_of, flip_of, active = offset_plan()
    pieces = []
    for number in range(49):
        matrix = level_couplings[int(slot_of[number])]
        if flip_of[number] == 1:
            matrix = matrix.T
        if active[number] == 0:
            matrix = jnp.zeros_like(matrix)
        pieces.append(matrix)
    return jnp.stack(pieces)

def matern_tiles(targets, sources, allowed):
    gap_rows = targets[:, 0][:, :, None] - sources[:, 0][:, None, :]
    gap_cols = targets[:, 1][:, :, None] - sources[:, 1][:, None, :]
    distance = jnp.sqrt(gap_rows * gap_rows + gap_cols * gap_cols)
    scaled = root_three * distance / length_scale
    variance = float(sources.shape[2]) ** (-0.5)
    kernel_value = (1.0 + scaled) * jnp.exp(-scaled) * variance
    return jnp.where(allowed[:, None, None], kernel_value, 0.0).astype(jnp.bfloat16)

def children_sum(transfer, coef):
    child_terms = jnp.einsum('xyrs,xyrc->xysc', transfer.astype(jnp.float32), coef.astype(jnp.float32))
    grid_rows, grid_cols = (coef.shape[0], coef.shape[1])
    shaped = child_terms.reshape(grid_rows // 2, 2, grid_cols // 2, 2, transfer.shape[3], coef.shape[3])
    return shaped.sum(axis=(1, 3))

def descend(transfer, parent):
    grid_rows, grid_cols = (parent.shape[0], parent.shape[1])
    shaped = transfer.reshape(grid_rows, 2, grid_cols, 2, transfer.shape[2], transfer.shape[3])
    spread = jnp.einsum('xaybrs,xysc->xaybrc', shaped.astype(jnp.float32), parent.astype(jnp.float32))
    return spread.reshape(2 * grid_rows, 2 * grid_cols, transfer.shape[2], parent.shape[3])

def far_level(coef, lists, couple_table):
    grid_rows, grid_cols = (lists.shape[0], lists.shape[1])
    padded = jnp.pad(coef, ((3, 3), (3, 3), (0, 0), (0, 0)))
    flattened = padded.reshape(-1, coef.shape[2], coef.shape[3])
    source_ids = lists.reshape(grid_rows * grid_cols, lists.shape[2])
    usable = source_ids >= 0
    clipped = jnp.maximum(source_ids, 0)
    source_row = clipped // grid_cols
    source_col = clipped % grid_cols
    cell_ids = jnp.arange(grid_rows * grid_cols, dtype=jnp.int32)
    target_row = (cell_ids // grid_cols)[:, None]
    target_col = (cell_ids % grid_cols)[:, None]
    offset_kind = jnp.clip((source_row - target_row + 3) * 7 + source_col - target_col + 3, 0, 48)
    located = (source_row + 3) * (grid_cols + 6) + source_col + 3

    def one_cell(packed):
        places, kind_here, allowed = packed
        matrices = jnp.where(allowed[:, None, None], couple_table[kind_here], jnp.zeros((), couple_table.dtype))
        return jnp.einsum('jrs,jsc->rc', matrices.astype(jnp.float32), flattened[places].astype(jnp.float32))
    result = lax.map(one_cell, (located, offset_kind, usable))
    return result.reshape(grid_rows, grid_cols, coef.shape[2], coef.shape[3])

def reference(positions, samples, leaf_basis, transfer_one, transfer_two, couplings, near_lists, far_zero, far_one, far_two):
    coef_zero = jnp.einsum('xypr,xypc->xyrc', leaf_basis.astype(jnp.float32), samples.astype(jnp.float32)).astype(jnp.bfloat16)
    coef_one = children_sum(transfer_one, coef_zero).astype(jnp.bfloat16)
    coef_two = children_sum(transfer_two, coef_one).astype(jnp.bfloat16)
    field_zero = far_level(coef_zero, far_zero, coupling_table(couplings[0]))
    field_one = far_level(coef_one, far_one, coupling_table(couplings[1]))
    field_two = far_level(coef_two, far_two, coupling_table(couplings[2]))
    down_two = field_two.astype(jnp.bfloat16)
    down_one = (field_one + descend(transfer_two, down_two)).astype(jnp.bfloat16)
    down_zero = (field_zero + descend(transfer_one, down_one)).astype(jnp.bfloat16)
    site_count = positions.shape[3]
    flat_samples = samples.reshape(-1, samples.shape[2], samples.shape[3])
    flat_positions = positions.reshape(-1, 2, site_count)
    near_ids = near_lists.reshape(-1, near_lists.shape[2])

    def one_leaf(packed):
        target, entries = packed
        allowed = entries >= 0
        clipped = jnp.maximum(entries, 0)
        kernel_tiles = matern_tiles(target[None], flat_positions[clipped], allowed)
        return jnp.einsum('jpq,jqc->pc', kernel_tiles.astype(jnp.float32), flat_samples[clipped].astype(jnp.float32))
    near_field = lax.map(one_leaf, (flat_positions, near_ids)).reshape(samples.shape)
    total_sum = near_field + jnp.einsum('xypr,xyrc->xypc', leaf_basis.astype(jnp.float32), down_zero.astype(jnp.float32))
    return total_sum.astype(jnp.bfloat16)
```

```python
import jax
import jax.numpy as jnp
from jax import lax
from jax.experimental import pallas as pl
from jax.experimental.pallas import tpu as pltpu
from jax.sharding import PartitionSpec as P

MESH = pl.DeviceIdType.MESH
bf16 = jnp.bfloat16
f32 = jnp.float32
LOG2E = 1.4426950408889634
LN2 = 0.6931471805599453
ROOT3 = 1.7320508075688772

HALF_INDEX = {}
for _u in range(0, 4):
    for _v in range(-3, 4):
        if max(abs(_u), abs(_v)) >= 2 and (_u > 0 or _v > 0):
            HALF_INDEX[(_u, _v)] = len(HALF_INDEX)


def nn(a, b):
    return jnp.dot(a, b, preferred_element_type=f32)


def nt(a, b):
    return lax.dot_general(a, b, (((1,), (1,)), ((), ())), preferred_element_type=f32)


def coupled(x, coup, level, u, v):
    if (u, v) in HALF_INDEX:
        return nt(x, coup[level, HALF_INDEX[(u, v)]])
    return nn(x, coup[level, HALF_INDEX[(-u, -v)]])


def far_pair(u, v):
    return max(abs(u), abs(v)) >= 2


def kernel(
    gx0,
    gy0,
    positions,
    samples,
    leaf_basis,
    transfer_one,
    transfer_two,
    couplings,
    near_lists,
    far_zero,
    far_one,
    far_two,
    out,
    basis,
    tone,
    ttwo,
    coup,
    pos,
    ext_s,
    ext_zero,
    ext_one,
    ext_two,
    field_zero,
    field_one,
    near_sum,
    part_zero,
    got_zero,
    part_one,
    got_one,
    part_two,
    got_two,
    part_near,
    got_near,
    mask_zero,
    mask_one,
    mask_two,
    own_two,
    mask_near,
    tiles,
    col_a,
    col_b,
    down_zero,
    staged,
    load_sem,
    pos_sem,
    out_sem,
    send,
    recv,
):
    X = lax.axis_index("qx")
    Y = lax.axis_index("qy")
    nx, ny = gx0 // 4, gy0 // 4
    px, py = lax.rem(X, 2), lax.rem(Y, 2)

    def at_x(k):
        return (lax.rem(X - px - 2 + k + nx, nx), Y)

    def at_y(k):
        return (X, lax.rem(Y - py - 2 + k + ny, ny))

    up, down = (lax.rem(X + nx - 1, nx), Y), (lax.rem(X + 1, nx), Y)
    left, right = (X, lax.rem(Y + ny - 1, ny)), (X, lax.rem(Y + 1, ny))

    def load(src, dst, n):
        return pltpu.make_async_copy(src, dst, load_sem.at[n])

    s_loads = [load(samples.at[r], ext_s.at[r, pl.ds(1, 4)], r) for r in range(4)]
    l_loads = [load(leaf_basis.at[r], basis.at[r], 4 + r) for r in range(4)]
    t_loads = [load(transfer_one, tone, 8), load(transfer_two, ttwo, 9)]
    c_loads = [load(couplings.at[l], coup.at[l], 10 + l) for l in range(3)]
    for r in range(4):
        s_loads[r].start()
        l_loads[r].start()

    def pos_copy(n):
        i, j = n // 6, lax.rem(n, 6)
        row = lax.rem(4 * X - 1 + i + gx0, gx0)
        col = lax.rem(4 * Y - 1 + j + gy0, gy0)
        return pltpu.make_async_copy(positions.at[row, col], pos.at[n], pos_sem.at[n])

    def start_pos(n, c):
        pos_copy(n).start()
        return c

    barrier = pltpu.get_barrier_semaphore()
    for k in range(6):

        @pl.when(k != 2 + px)
        def _():
            pl.semaphore_signal(barrier, inc=1, device_id=at_x(k), device_id_type=MESH)

        @pl.when(k != 2 + py)
        def _():
            pl.semaphore_signal(barrier, inc=1, device_id=at_y(k), device_id_type=MESH)

    for c in t_loads + c_loads:
        c.start()
    lax.fori_loop(0, 36, start_pos, 0)

    def mask_of(lst, row0, col0, rows, grid_rows, grid_cols, width):
        k = lax.broadcasted_iota(jnp.int32, (rows, 1), 0)
        b = k & 7
        r, c = row0 + (k >> 3), col0 + b
        ok = (r >= 0) & (r < grid_rows) & (c >= 0) & (c < grid_cols) & (b < width)
        ident = jnp.where(ok, r * grid_cols + c, -2)
        hit = jnp.max(jnp.where(ident == lst, 1.0, 0.0), axis=1, keepdims=True)
        return jnp.broadcast_to(hit, (rows, 128))

    for i in range(4):
        for j in range(4):
            r0, c0 = 4 * X + 2 * (i // 2) - 2, 4 * Y + 2 * (j // 2) - 2
            mask_zero[i + 2, j] = mask_of(far_zero[i, j : j + 1, :], r0, c0, 48, gx0, gy0, 6)
            mask_near[i + 1, j] = mask_of(
                near_lists[i, j : j + 1, :], 4 * X + i - 1, 4 * Y + j - 1, 24, gx0, gy0, 3
            )
    for i in range(2):
        for j in range(2):
            mask_one[i + 2, j] = mask_of(
                far_one[i, j : j + 1, :], 2 * X - 2, 2 * Y - 2, 48, gx0 // 2, gy0 // 2, 6
            )
    own_two[...] = mask_of(
        far_two[0, 0:1, :], X - px - 2, Y - py - 2, 48, gx0 // 4, gy0 // 4, 6
    )

    pl.semaphore_wait(barrier, 10)

    def remote(src, dst, n, dev):
        return pltpu.make_async_remote_copy(
            src_ref=src,
            dst_ref=dst,
            send_sem=send.at[n],
            recv_sem=recv.at[n],
            device_id=dev,
            device_id_type=MESH,
        )

    x_samples = [
        remote(samples.at[:, 3], ext_s.at[:, 0], 0, right),
        remote(samples.at[:, 0], ext_s.at[:, 5], 1, left),
    ]
    rows_lo, rows_hi = pl.ds(0, 16), pl.ds(32, 16)
    x_masks = [
        remote(mask_zero.at[pl.ds(4, 2), :, rows_hi], mask_zero.at[pl.ds(0, 2), :, rows_hi], 2, down),
        remote(mask_zero.at[pl.ds(2, 2), :, rows_lo], mask_zero.at[pl.ds(6, 2), :, rows_lo], 3, up),
        remote(mask_one.at[pl.ds(2, 2), :, rows_hi], mask_one.at[pl.ds(0, 2), :, rows_hi], 4, down),
        remote(mask_one.at[pl.ds(2, 2), :, rows_lo], mask_one.at[pl.ds(4, 2), :, rows_lo], 5, up),
        remote(mask_near.at[4, :, pl.ds(16, 8)], mask_near.at[0, :, pl.ds(16, 8)], 6, down),
        remote(mask_near.at[1, :, pl.ds(0, 8)], mask_near.at[5, :, pl.ds(0, 8)], 7, up),
    ]
    for c in x_samples + x_masks:
        c.start()

    def x_mask_two(k):
        slot = px + 4 - 2 * (k // 2)
        return pltpu.make_async_remote_copy(
            src_ref=own_two.at[pl.ds(8 * k, 8)],
            dst_ref=mask_two.at[slot],
            send_sem=send.at[40 + k],
            recv_sem=recv.at[40 + slot],
            device_id=at_x(k),
            device_id_type=MESH,
        )

    def x_two(k):
        slot = py + 4 - 2 * (k // 2)
        return pltpu.make_async_remote_copy(
            src_ref=ext_two.at[2 + py],
            dst_ref=ext_two.at[slot],
            send_sem=send.at[46 + k],
            recv_sem=recv.at[46 + slot],
            device_id=at_y(k),
            device_id_type=MESH,
        )

    def x_part_two(k):
        slot = px + 4 - 2 * (k // 2)
        return pltpu.make_async_remote_copy(
            src_ref=part_two.at[k],
            dst_ref=got_two.at[slot],
            send_sem=send.at[52 + k],
            recv_sem=recv.at[52 + slot],
            device_id=at_x(k),
            device_id_type=MESH,
        )

    def recv_wait(dst, n):
        pltpu.make_async_copy(dst, dst, recv.at[n]).wait()

    for k in range(6):

        @pl.when(k != 2 + px)
        def _():
            x_mask_two(k).start()

    mask_two[2 + px] = own_two[pl.ds(pl.multiple_of(8 * (2 + px), 8), 8), :]

    x_zero = []
    for r in range(4):
        s_loads[r].wait()
        l_loads[r].wait()
        for j in range(4):
            ext_zero[r, 2 + j] = nn(ext_s[r, 1 + j].T, basis[r, j]).astype(bf16)
        x_zero.append(
            remote(ext_zero.at[r, pl.ds(4, 2)], ext_zero.at[r, pl.ds(0, 2)], 8 + 2 * r, right)
        )
        x_zero.append(
            remote(ext_zero.at[r, pl.ds(2, 2)], ext_zero.at[r, pl.ds(6, 2)], 9 + 2 * r, left)
        )
        x_zero[-2].start()
        x_zero[-1].start()

    t_loads[0].wait()
    x_one = []
    for i in range(2):
        for j in range(2):
            total = None
            for a in range(2):
                for b in range(2):
                    term = nn(ext_zero[2 * i + a, 2 + 2 * j + b], tone[2 * i + a, 2 * j + b])
                    total = term if total is None else total + term
            ext_one[i, 2 + j] = total.astype(bf16)
        x_one.append(remote(ext_one.at[i, pl.ds(2, 2)], ext_one.at[i, pl.ds(0, 2)], 16 + 2 * i, right))
        x_one.append(remote(ext_one.at[i, pl.ds(2, 2)], ext_one.at[i, pl.ds(4, 2)], 17 + 2 * i, left))
        x_one[-2].start()
        x_one[-1].start()

    t_loads[1].wait()
    total = None
    for a in range(2):
        for b in range(2):
            term = nn(ext_one[a, 2 + b], ttwo[a, b])
            total = term if total is None else total + term
    ext_two[2 + py] = total.astype(bf16)
    for k in range(6):

        @pl.when(k != 2 + py)
        def _():
            x_two(k).start()

    def wait_pos(n, c):
        pos_copy(n).wait()
        return c

    lax.fori_loop(0, 36, wait_pos, 0)
    pos[...] = pos[...] * (ROOT3 * LOG2E)

    def near_target(i, j, first, count, store):
        here = pos[i * 6 + j + 1]
        col_a[...] = jnp.broadcast_to(here[0:1], (128, 256)).T
        col_b[...] = jnp.broadcast_to(here[1:2], (128, 256)).T
        for q in range(count):
            for b in range(3):
                sr = first + q
                there = pos[(sr + 1) * 6 + j + b]
                xs, ys = there[0:1], there[1:2]
                mask = mask_near[i, j, pl.ds((sr - i + 2) * 8 + b, 1), :]
                c0, c1 = mask * 0.0625, mask * (0.0625 * LN2)
                for h in range(2):
                    lanes = slice(128 * h, 128 * h + 128)
                    for w in range(8):
                        span = slice(32 * w, 32 * w + 32)
                        dx = col_a[span, :] - xs[:, lanes]
                        dy = col_b[span, :] - ys[:, lanes]
                        d2 = jnp.maximum(dx * dx + dy * dy, 1e-30)
                        d = d2 * lax.rsqrt(d2)
                        value = (c0 + c1 * d) * jnp.exp2(-d)
                        tiles[q * 3 + b, span, lanes] = value.astype(bf16)
        total = None
        for q in range(count):
            for b in range(3):
                term = nn(tiles[q * 3 + b], ext_s[first + q, j + b])
                total = term if total is None else total + term
        store(total)

    def near_columns(column):
        def middle(n, c):
            i, j = n // 2, column(lax.rem(n, 2))

            def store(v):
                near_sum[i + 1, j] = v

            near_target(i + 2, j, i, 3, store)
            return c

        def edge(n, c):
            e, j = n // 2, column(lax.rem(n, 2))

            def store(v):
                near_sum[3 * e, j] = v

            near_target(3 * e + 1, j, 2 * e, 2, store)
            return c

        def outer(n, c):
            e, j = n // 2, column(lax.rem(n, 2))

            def store(v):
                part_near[e, j] = v.astype(bf16)

            near_target(5 * e, j, 3 * e, 1, store)
            return c

        lax.fori_loop(0, 4, outer, 0)
        lax.fori_loop(0, 4, middle, 0)
        lax.fori_loop(0, 4, edge, 0)

    for c in x_masks:
        c.wait()
    near_columns(lambda q: q + 1)
    for c in x_samples:
        c.wait()
    near_columns(lambda q: 3 * q)
    x_near = [
        remote(part_near.at[0], got_near.at[1], 20, up),
        remote(part_near.at[1], got_near.at[0], 21, down),
    ]
    for c in x_near:
        c.start()

    for c in c_loads:
        c.wait()
    for c in x_zero:
        c.wait()

    def far_zero_row(i):
        if i < 0:
            rows, shift = (0, 1), 4
        elif i > 3:
            rows, shift = (2, 3), -2
        else:
            rows, shift = (0, 1, 2, 3), (2 if i < 2 else 0)
        for p in range(2):

            def body(h, c):
                j = 2 * h + p
                total = None
                for sr in rows:
                    for b in range(6):
                        u, v = sr - i, b - 2 - p
                        if not far_pair(u, v):
                            continue
                        m = mask_zero[i + 2, j, pl.ds((sr + shift) * 8 + b, 1), :]
                        m = jnp.concatenate([m, m], axis=1).astype(bf16)
                        term = coupled(ext_zero[sr, 2 * h + b] * m, coup, 0, u, v)
                        total = term if total is None else total + term
                if i < 0:
                    part_zero[i + 2, j] = total.astype(bf16)
                elif i > 3:
                    part_zero[i - 2, j] = total.astype(bf16)
                else:
                    field_zero[i, j] = total
                return c

            lax.fori_loop(0, 2, body, 0)

    far_zero_row(-2)
    far_zero_row(-1)
    x_far = [remote(part_zero.at[pl.ds(0, 2)], got_zero.at[pl.ds(2, 2)], 22, up)]
    x_far[0].start()
    far_zero_row(4)
    far_zero_row(5)
    x_far.append(remote(part_zero.at[pl.ds(2, 2)], got_zero.at[pl.ds(0, 2)], 23, down))
    x_far[1].start()
    for i in range(4):
        far_zero_row(i)

    for c in x_one:
        c.wait()

    def far_one_row(i):
        for j in range(2):
            total = None
            for sr in range(2):
                for b in range(6):
                    u, v = sr - i, b - 2 - j
                    if not far_pair(u, v):
                        continue
                    a = sr + 2 if 0 <= i < 2 else (sr + 4 if i < 0 else sr)
                    m = mask_one[i + 2, j, pl.ds(a * 8 + b, 1), :]
                    m = jnp.concatenate([m, m], axis=1).astype(bf16)
                    term = coupled(ext_one[sr, b] * m, coup, 1, u, v)
                    total = term if total is None else total + term
            if i < 0:
                part_one[0, i + 2, j] = total.astype(bf16)
            elif i > 1:
                part_one[1, i - 2, j] = total.astype(bf16)
            else:
                field_one[i, j] = total

    far_one_row(-2)
    far_one_row(-1)
    x_far.append(remote(part_one.at[0], got_one.at[1], 24, up))
    x_far[2].start()
    far_one_row(2)
    far_one_row(3)
    x_far.append(remote(part_one.at[1], got_one.at[0], 25, down))
    x_far[3].start()

    for k in range(6):

        @pl.when(k != 2 + py)
        def _():
            x_two(k).wait_send()
            recv_wait(ext_two.at[k], 46 + k)

        @pl.when(k != 2 + px)
        def _():
            x_mask_two(k).wait_send()
            recv_wait(mask_two.at[k], 40 + k)

    for qx in range(2):
        for qy in range(2):

            @pl.when((px == qx) & (py == qy))
            def _():
                for k in range(6):
                    u = qx + 2 - k
                    total = None
                    for b in range(6):
                        v = b - 2 - qy
                        if not far_pair(u, v):
                            continue
                        m = mask_two[k, pl.ds(b, 1), :]
                        m = jnp.concatenate([m, m], axis=1).astype(bf16)
                        term = coupled(ext_two[b] * m, coup, 2, u, v)
                        total = term if total is None else total + term
                    part_two[k] = total.astype(bf16)

    for k in range(6):

        @pl.when(k != 2 + px)
        def _():
            x_part_two(k).start()

    far_one_row(0)
    far_one_row(1)

    for k in range(6):

        @pl.when(k != 2 + px)
        def _():
            x_part_two(k).wait_send()
            recv_wait(got_two.at[k], 52 + k)

    got_two[2 + px] = part_two[2 + px]
    total = got_two[0].astype(f32)
    for k in range(1, 6):
        total += got_two[k].astype(f32)
    down_two = total.astype(bf16)
    for c in x_far:
        c.wait()
    for c in x_near:
        c.wait()
    down_one = []
    for i in range(2):
        for j in range(2):
            value = field_one[i, j] + nt(down_two, ttwo[i, j])
            value += got_one[0, i, j].astype(f32) + got_one[1, i, j].astype(f32)
            part_one[0, i, j] = value.astype(bf16)

    def descend(n, c):
        i, h = n // 2, lax.rem(n, 2)
        for b in range(2):
            j = 2 * h + b
            value = field_zero[i, j] + nt(part_one[0, i // 2, h], tone[i, j])
            down_zero[i, j] = (value + got_zero[i, j].astype(f32)).astype(bf16)
        return c

    lax.fori_loop(0, 8, descend, 0)

    for e in range(2):
        for j in range(4):
            near_sum[3 * e, j] += got_near[e, j].astype(f32)

    def finish(i, c):
        for j in range(4):
            staged[i, j] = (near_sum[i, j] + nt(basis[i, j], down_zero[i, j])).astype(bf16)
        pltpu.make_async_copy(staged.at[i], out.at[i], out_sem.at[i]).start()
        return c

    lax.fori_loop(0, 4, finish, 0)

    def drain(i, c):
        pltpu.make_async_copy(staged.at[i], out.at[i], out_sem.at[i]).wait()
        return c

    lax.fori_loop(0, 4, drain, 0)


def solution(mesh):
    nx, ny = mesh.shape["qx"], mesh.shape["qy"]

    def per_device(
        positions,
        samples,
        leaf_basis,
        transfer_one,
        transfer_two,
        couplings,
        near_lists,
        far_zero,
        far_one,
        far_two,
    ):
        def body(*refs):
            kernel(4 * nx, 4 * ny, *refs)

        hbm = pl.BlockSpec(memory_space=pl.ANY)
        vmem = pl.BlockSpec(memory_space=pltpu.VMEM)
        block = (256, 256)
        return pl.pallas_call(
            body,
            out_shape=jax.ShapeDtypeStruct(samples.shape, bf16),
            in_specs=[hbm] * 6 + [vmem] * 4,
            out_specs=hbm,
            scratch_shapes=[
                pltpu.VMEM((4, 4) + block, bf16),
                pltpu.VMEM((4, 4) + block, bf16),
                pltpu.VMEM((2, 2) + block, bf16),
                pltpu.VMEM((3, 20) + block, bf16),
                pltpu.VMEM((36, 2, 256), f32),
                pltpu.VMEM((4, 6) + block, bf16),
                pltpu.VMEM((4, 8) + block, bf16),
                pltpu.VMEM((2, 6) + block, bf16),
                pltpu.VMEM((6,) + block, bf16),
                pltpu.VMEM((4, 4) + block, f32),
                pltpu.VMEM((2, 2) + block, f32),
                pltpu.VMEM((4, 4) + block, f32),
                pltpu.VMEM((4, 4) + block, bf16),
                pltpu.VMEM((4, 4) + block, bf16),
                pltpu.VMEM((2, 2, 2) + block, bf16),
                pltpu.VMEM((2, 2, 2) + block, bf16),
                pltpu.VMEM((6,) + block, bf16),
                pltpu.VMEM((6,) + block, bf16),
                pltpu.VMEM((2, 4) + block, bf16),
                pltpu.VMEM((2, 4) + block, bf16),
                pltpu.VMEM((8, 4, 48, 128), f32),
                pltpu.VMEM((6, 2, 48, 128), f32),
                pltpu.VMEM((6, 8, 128), f32),
                pltpu.VMEM((48, 128), f32),
                pltpu.VMEM((6, 4, 24, 128), f32),
                pltpu.VMEM((9,) + block, bf16),
                pltpu.VMEM((256, 128), f32),
                pltpu.VMEM((256, 128), f32),
                pltpu.VMEM((4, 4) + block, bf16),
                pltpu.VMEM((4, 4) + block, bf16),
                pltpu.SemaphoreType.DMA((13,)),
                pltpu.SemaphoreType.DMA((36,)),
                pltpu.SemaphoreType.DMA((4,)),
                pltpu.SemaphoreType.DMA((58,)),
                pltpu.SemaphoreType.DMA((58,)),
            ],
            compiler_params=pltpu.CompilerParams(
                collective_id=0, has_side_effects=True, vmem_limit_bytes=60 << 20
            ),
        )(
            positions,
            samples,
            leaf_basis,
            transfer_one,
            transfer_two,
            couplings,
            near_lists,
            far_zero,
            far_one,
            far_two,
        )

    cell = P("qx", "qy", None, None)
    short = P("qx", "qy", None)
    return jax.shard_map(
        per_device,
        mesh=mesh,
        in_specs=(P(), cell, cell, cell, cell, P(), short, short, short, short),
        out_specs=cell,
        check_vma=False,
    )
```

```python
import jax
import jax.numpy as jnp
from jax import lax
from jax.experimental import pallas as pl
from jax.experimental.pallas import tpu as pltpu
from jax.sharding import PartitionSpec as P

MESH = pl.DeviceIdType.MESH
bf16 = jnp.bfloat16
f32 = jnp.float32
LOG2E = 1.4426950408889634
LN2 = 0.6931471805599453
ROOT3 = 1.7320508075688772

HALF_INDEX = {}
for _u in range(0, 4):
    for _v in range(-3, 4):
        if max(abs(_u), abs(_v)) >= 2 and (_u > 0 or _v > 0):
            HALF_INDEX[(_u, _v)] = len(HALF_INDEX)


def nn(a, b):
    return jnp.dot(a, b, preferred_element_type=f32)


def nt(a, b):
    return lax.dot_general(a, b, (((1,), (1,)), ((), ())), preferred_element_type=f32)


def coupled(x, coup, level, u, v):
    if (u, v) in HALF_INDEX:
        return nt(x, coup[level, HALF_INDEX[(u, v)]])
    return nn(x, coup[level, HALF_INDEX[(-u, -v)]])


def far_pair(u, v):
    return max(abs(u), abs(v)) >= 2


def kernel(
    gx0,
    gy0,
    positions,
    samples,
    leaf_basis,
    transfer_one,
    transfer_two,
    couplings,
    near_lists,
    far_zero,
    far_one,
    far_two,
    out,
    basis,
    tone,
    ttwo,
    coup,
    pos,
    ext_s,
    ext_zero,
    ext_one,
    ext_two,
    field_zero,
    field_one,
    near_sum,
    part_zero,
    got_zero,
    part_one,
    got_one,
    part_two,
    got_two,
    part_near,
    got_near,
    mask_zero,
    mask_one,
    mask_two,
    own_two,
    mask_near,
    tiles,
    cols,
    half_zero,
    edge_near,
    down_zero,
    load_sem,
    pos_sem,
    out_sem,
    send,
    recv,
):
    X = lax.axis_index("qx")
    Y = lax.axis_index("qy")
    nx, ny = gx0 // 4, gy0 // 4
    px, py = lax.rem(X, 2), lax.rem(Y, 2)

    def at_x(k):
        return (lax.rem(X - px - 2 + k + nx, nx), Y)

    def at_y(k):
        return (X, lax.rem(Y - py - 2 + k + ny, ny))

    up, down = (lax.rem(X + nx - 1, nx), Y), (lax.rem(X + 1, nx), Y)
    left, right = (X, lax.rem(Y + ny - 1, ny)), (X, lax.rem(Y + 1, ny))

    def load(src, dst, n):
        return pltpu.make_async_copy(src, dst, load_sem.at[n])

    s_loads = [load(samples.at[r], ext_s.at[r, pl.ds(1, 4)], r) for r in range(4)]
    l_loads = [load(leaf_basis.at[r], basis.at[r], 4 + r) for r in range(4)]
    t_loads = [load(transfer_one, tone, 8), load(transfer_two, ttwo, 9)]
    c_loads = [load(couplings.at[l], coup.at[l], 10 + l) for l in range(3)]
    for r in range(4):
        s_loads[r].start()
        l_loads[r].start()

    def pos_copy(n):
        i, j = n // 6, lax.rem(n, 6)
        row = lax.rem(4 * X - 1 + i + gx0, gx0)
        col = lax.rem(4 * Y - 1 + j + gy0, gy0)
        return pltpu.make_async_copy(positions.at[row, col], pos.at[n], pos_sem.at[n])

    def start_pos(n, c):
        pos_copy(n).start()
        return c

    barrier = pltpu.get_barrier_semaphore()
    for k in range(6):

        @pl.when(k != 2 + px)
        def _():
            pl.semaphore_signal(barrier, inc=1, device_id=at_x(k), device_id_type=MESH)

        @pl.when(k != 2 + py)
        def _():
            pl.semaphore_signal(barrier, inc=1, device_id=at_y(k), device_id_type=MESH)

    for c in t_loads + c_loads:
        c.start()
    lax.fori_loop(0, 36, start_pos, 0)

    def mask_of(lst, row0, col0, rows, grid_rows, grid_cols, width):
        k = lax.broadcasted_iota(jnp.int32, (rows, 1), 0)
        b = k & 7
        r, c = row0 + (k >> 3), col0 + b
        ok = (r >= 0) & (r < grid_rows) & (c >= 0) & (c < grid_cols) & (b < width)
        ident = jnp.where(ok, r * grid_cols + c, -2)
        hit = jnp.max(jnp.where(ident == lst, 1.0, 0.0), axis=1, keepdims=True)
        return jnp.broadcast_to(hit, (rows, 128))

    for i in range(4):
        for j in range(4):
            r0, c0 = 4 * X + 2 * (i // 2) - 2, 4 * Y + 2 * (j // 2) - 2
            mask_zero[i + 2, j] = mask_of(far_zero[i, j : j + 1, :], r0, c0, 48, gx0, gy0, 6)
            mask_near[i + 1, j] = mask_of(
                near_lists[i, j : j + 1, :], 4 * X + i - 1, 4 * Y + j - 1, 24, gx0, gy0, 3
            )
    for i in range(2):
        for j in range(2):
            mask_one[i + 2, j] = mask_of(
                far_one[i, j : j + 1, :], 2 * X - 2, 2 * Y - 2, 48, gx0 // 2, gy0 // 2, 6
            )
    own_two[...] = mask_of(
        far_two[0, 0:1, :], X - px - 2, Y - py - 2, 48, gx0 // 4, gy0 // 4, 6
    )

    pl.semaphore_wait(barrier, 10)

    def remote(src, dst, n, dev):
        return pltpu.make_async_remote_copy(
            src_ref=src,
            dst_ref=dst,
            send_sem=send.at[n],
            recv_sem=recv.at[n],
            device_id=dev,
            device_id_type=MESH,
        )

    x_samples = []
    for half in range(2):
        rows = pl.ds(2 * px if half == 0 else 2 - 2 * px, 2)
        x_samples += [
            remote(samples.at[rows, 3], ext_s.at[rows, 0], 30 * half, right),
            remote(samples.at[rows, 0], ext_s.at[rows, 5], 30 * half + 1, left),
        ]
    x_samples[0].start()
    x_samples[1].start()
    rows_lo, rows_hi = pl.ds(0, 16), pl.ds(32, 16)
    x_masks = [
        remote(mask_zero.at[pl.ds(4, 2), :, rows_hi], mask_zero.at[pl.ds(0, 2), :, rows_hi], 2, down),
        remote(mask_zero.at[pl.ds(2, 2), :, rows_lo], mask_zero.at[pl.ds(6, 2), :, rows_lo], 3, up),
        remote(mask_one.at[pl.ds(2, 2), :, rows_hi], mask_one.at[pl.ds(0, 2), :, rows_hi], 4, down),
        remote(mask_one.at[pl.ds(2, 2), :, rows_lo], mask_one.at[pl.ds(4, 2), :, rows_lo], 5, up),
        remote(mask_near.at[4, :, pl.ds(16, 8)], mask_near.at[0, :, pl.ds(16, 8)], 6, down),
        remote(mask_near.at[1, :, pl.ds(0, 8)], mask_near.at[5, :, pl.ds(0, 8)], 7, up),
    ]
    for c in x_masks:
        c.start()

    def x_mask_two(k):
        slot = px + 4 - 2 * (k // 2)
        return pltpu.make_async_remote_copy(
            src_ref=own_two.at[pl.ds(8 * k, 8)],
            dst_ref=mask_two.at[slot],
            send_sem=send.at[40 + k],
            recv_sem=recv.at[40 + slot],
            device_id=at_x(k),
            device_id_type=MESH,
        )

    def x_two(k):
        source, slot, dev = (
            (2 + py, 2 - py, right),
            (2 + py, 4 - py, left),
            (1 + py, 1 - py, right),
            (3 + py, 5 - py, left),
            (5 * py, 5 * py, (X, Y + 1 - 2 * py)),
        )[k]
        return pltpu.make_async_remote_copy(
            src_ref=ext_two.at[source],
            dst_ref=ext_two.at[slot],
            send_sem=send.at[46 + k],
            recv_sem=recv.at[46 + slot],
            device_id=dev,
            device_id_type=MESH,
        )

    def x_part_two(k):
        slot = px + 4 - 2 * (k // 2)
        return pltpu.make_async_remote_copy(
            src_ref=part_two.at[k],
            dst_ref=got_two.at[slot],
            send_sem=send.at[52 + k],
            recv_sem=recv.at[52 + slot],
            device_id=at_x(k),
            device_id_type=MESH,
        )

    def recv_wait(dst, n):
        pltpu.make_async_copy(dst, dst, recv.at[n]).wait()

    for k in range(6):

        @pl.when(k != 2 + px)
        def _():
            x_mask_two(k).start()

    mask_two[2 + px] = own_two[pl.ds(pl.multiple_of(8 * (2 + px), 8), 8), :]

    x_zero = []
    for r in range(4):
        s_loads[r].wait()
        l_loads[r].wait()
        for j in range(4):
            ext_zero[r, 2 + j] = nn(ext_s[r, 1 + j].T, basis[r, j]).astype(bf16)
    for q in range(4):
        r = lax.rem(q + 2 * px, 4)
        x_zero += [
            remote(ext_zero.at[r, pl.ds(4, 2)], ext_zero.at[r, pl.ds(0, 2)], 8 + 2 * q, right),
            remote(ext_zero.at[r, pl.ds(2, 2)], ext_zero.at[r, pl.ds(6, 2)], 9 + 2 * q, left),
        ]

    t_loads[0].wait()
    x_one = []
    for i in range(2):
        for j in range(2):
            total = None
            for a in range(2):
                for b in range(2):
                    term = nn(ext_zero[2 * i + a, 2 + 2 * j + b], tone[2 * i + a, 2 * j + b])
                    total = term if total is None else total + term
            ext_one[i, 2 + j] = total.astype(bf16)
        x_one.append(remote(ext_one.at[i, pl.ds(2, 2)], ext_one.at[i, pl.ds(0, 2)], 16 + 2 * i, right))
        x_one.append(remote(ext_one.at[i, pl.ds(2, 2)], ext_one.at[i, pl.ds(4, 2)], 17 + 2 * i, left))

    t_loads[1].wait()
    total = None
    for a in range(2):
        for b in range(2):
            term = nn(ext_one[a, 2 + b], ttwo[a, b])
            total = term if total is None else total + term
    ext_two[2 + py] = total.astype(bf16)
    x_two(0).start()
    x_two(1).start()
    x_zero[0].start()
    x_zero[1].start()

    def wait_pos(n, c):
        pos_copy(n).wait()
        return c

    lax.fori_loop(0, 36, wait_pos, 0)
    pos[...] = pos[...] * (ROOT3 * LOG2E)

    for c in x_masks:
        c.wait()
    c_loads[0].wait()

    def zero_rows(i):
        if i < 0:
            return (0, 1), 4
        if i > 3:
            return (2, 3), -2
        return (0, 1, 2, 3), (2 if i < 2 else 0)

    def zero_terms(i, j, halo):
        rows, shift = zero_rows(i)
        for sr in rows:
            for b in range(6):
                column = 2 * (j // 2) + b
                u, v = sr - i, b - 2 - j % 2
                if far_pair(u, v) and halo == (not 2 <= column < 6):
                    yield sr, column, u, v, (sr + shift) * 8 + b

    def zero_term(i, j, sr, column, u, v, row):
        m = mask_zero[i + 2, j, pl.ds(row, 1), :]
        m = jnp.concatenate([m, m], axis=1).astype(bf16)
        return coupled(ext_zero[sr, column] * m, coup, 0, u, v)

    def zero_work(targets):
        for i, j in targets:
            total = None
            for term in zero_terms(i, j, False):
                if total is not None:
                    yield True
                value = zero_term(i, j, *term)
                total = value if total is None else total + value
            if 0 <= i < 4:
                field_zero[i, j] = total
            else:
                half_zero[i + 2 if i < 0 else i - 2, j] = total
            yield False

    halo_tile = {}

    def near_sources(i, j):
        for sr in range(max(i - 1, 0), min(i + 1, 3) + 1):
            for b in range(3):
                yield sr, j + b

    jobs = [(i, j) for i in (-1, 4, 0, 1, 2, 3) for j in range(4)]

    def make_tile(target, slot, i, j, sr, column):
        there = pos[(sr + 1) * 6 + column]
        xs, ys = there[0:1], there[1:2]
        mask = mask_near[i + 1, j, pl.ds((sr - i + 1) * 8 + column - j, 1), :]
        c0, c1 = mask * 0.0625, mask * (0.0625 * LN2)
        for h in range(2):
            lanes = slice(128 * h, 128 * h + 128)
            for w in range(4):
                span = slice(64 * w, 64 * w + 64)
                dx = cols[target, 0, span, :] - xs[:, lanes]
                dy = cols[target, 1, span, :] - ys[:, lanes]
                d2 = jnp.maximum(dx * dx + dy * dy, 1e-30)
                d = d2 * lax.rsqrt(d2)
                value = (c0 + c1 * d) * jnp.exp2(-d)
                tiles[slot, span, lanes] = value.astype(bf16)

    def near_work(i, j, terms):
        total = None
        for slot, sr, column in terms:
            value = nn(tiles[slot], ext_s[sr, column])
            total = value if total is None else total + value
            yield
        if 0 <= i < 4:
            near_sum[i, j] = total
        elif j in (1, 2):
            part_near[0 if i < 0 else 1, j] = total.astype(bf16)
        else:
            edge_near[0 if i < 0 else 1, j // 2] = total

    def level_two():
        c_loads[2].wait()
        for k in range(5):
            x_two(k).wait_send()
        recv_wait(ext_two.at[5 - 5 * py], 51 - 5 * py)
        for k in range(6):

            @pl.when(k != 2 + px)
            def _():
                x_mask_two(k).wait_send()
                recv_wait(mask_two.at[k], 40 + k)

        for qy in range(2):
            for u in range(-3, 4):
                k = px + 2 - u

                @pl.when((py == qy) & (k >= 0) & (k < 6))
                def _():
                    total = None
                    for b in range(6):
                        v = b - 2 - qy
                        if not far_pair(u, v):
                            continue
                        m = mask_two[k, pl.ds(b, 1), :]
                        m = jnp.concatenate([m, m], axis=1).astype(bf16)
                        term = coupled(ext_two[b] * m, coup, 2, u, v)
                        total = term if total is None else total + term
                    part_two[k] = total.astype(bf16)

        for k in range(6):

            @pl.when(k != 2 + px)
            def _():
                x_part_two(k).start()

    def halo_row(i):
        for j in range(4):
            if i < 0:
                total = half_zero[i + 2, j]
            elif i > 3:
                total = half_zero[i - 2, j]
            else:
                total = field_zero[i, j]
            for term in zero_terms(i, j, True):
                total += zero_term(i, j, *term)
            if i < 0:
                part_zero[i + 2, j] = total.astype(bf16)
            elif i > 3:
                part_zero[i - 2, j] = total.astype(bf16)
            else:
                field_zero[i, j] = total

    x_far = [
        remote(part_zero.at[pl.ds(0, 2)], got_zero.at[pl.ds(2, 2)], 22, up),
        remote(part_zero.at[pl.ds(2, 2)], got_zero.at[pl.ds(0, 2)], 23, down),
    ]

    def far_edge(e):
        for i in ((-2, -1), (4, 5))[e]:
            halo_row(i)
        x_far[e].start()

    x_near = [
        remote(part_near.at[0], got_near.at[1], 20, up),
        remote(part_near.at[1], got_near.at[0], 21, down),
    ]

    def near_edge(e):
        for side in range(2):
            j, column = 3 * side, 5 * side
            value = nn(tiles[halo_tile[(5 * e - 1, j, 3 * e)]], ext_s[3 * e, column])
            part_near[e, j] = (edge_near[e, side] + value).astype(bf16)
        x_near[e].start()

    far_order = [(i, j) for i in (-2, -1, 4, 5, 0, 1, 2, 3) for j in range(4)]
    count = sum(1 for i, j in jobs for _ in near_sources(i, j))
    rate = sum(1 for i, j in far_order for _ in zero_terms(i, j, False)) / count
    far, before, owed = zero_work(far_order), iter(()), 0.0
    for n, (i, j) in enumerate(jobs):
        here = pos[(i + 1) * 6 + j + 1]
        cols[n % 2, 0] = jnp.broadcast_to(here[0:1], (128, 256)).T
        cols[n % 2, 1] = jnp.broadcast_to(here[1:2], (128, 256)).T
        terms = []
        for q, (sr, column) in enumerate(near_sources(i, j)):
            if 1 <= column < 5:
                slot = 9 * (n % 2) + q
                terms.append((slot, sr, column))
            else:
                slot = 18 + len(halo_tile)
                halo_tile[(i, j, sr)] = slot
            make_tile(n % 2, slot, i, j, sr, column)
            owed += rate
            while owed >= 1.0:
                next(far, None)
                owed -= 1.0
            next(before, None)
        for _ in before:
            pass
        before = near_work(i, j, terms)
        if n == 4:
            recv_wait(ext_two.at[1 + py], 47 + py)
            recv_wait(ext_two.at[3 + py], 49 + py)
            x_two(2).start()
            x_two(3).start()
            x_zero[2].start()
            x_zero[3].start()
        if n == 11:
            recv_wait(ext_two.at[py], 46 + py)
            recv_wait(ext_two.at[4 + py], 50 + py)
            x_two(4).start()
            for c in x_zero[4:] + x_one + x_samples[2:]:
                c.start()
        if n in (13, 16):
            while next(far, False):
                owed -= 1.0
        if n == 13:
            level_two()
            for c in x_samples[:2]:
                c.wait()
            for e in range(2):

                @pl.when(px == e)
                def _():
                    near_edge(e)

        if n == 16:
            for c in x_zero[:4]:
                c.wait()
            for e in range(2):

                @pl.when(px == e)
                def _():
                    far_edge(e)

    for _ in before:
        pass
    for _ in far:
        pass

    for c in x_zero[4:]:
        c.wait()
    for e in range(2):

        @pl.when(px != e)
        def _():
            far_edge(e)

    for i in range(4):
        halo_row(i)

    c_loads[1].wait()
    for c in x_one:
        c.wait()

    def far_one_row(i):
        for j in range(2):
            total = None
            for sr in range(2):
                for b in range(6):
                    u, v = sr - i, b - 2 - j
                    if not far_pair(u, v):
                        continue
                    a = sr + 2 if 0 <= i < 2 else (sr + 4 if i < 0 else sr)
                    m = mask_one[i + 2, j, pl.ds(a * 8 + b, 1), :]
                    m = jnp.concatenate([m, m], axis=1).astype(bf16)
                    term = coupled(ext_one[sr, b] * m, coup, 1, u, v)
                    total = term if total is None else total + term
            if i < 0:
                part_one[0, i + 2, j] = total.astype(bf16)
            elif i > 1:
                part_one[1, i - 2, j] = total.astype(bf16)
            else:
                field_one[i, j] = total

    far_one_row(-2)
    far_one_row(-1)
    x_far.append(remote(part_one.at[0], got_one.at[1], 24, up))
    x_far[2].start()
    far_one_row(2)
    far_one_row(3)
    x_far.append(remote(part_one.at[1], got_one.at[0], 25, down))
    x_far[3].start()

    far_one_row(0)
    far_one_row(1)

    for k in range(6):

        @pl.when(k != 2 + px)
        def _():
            x_part_two(k).wait_send()
            recv_wait(got_two.at[k], 52 + k)

    got_two[2 + px] = part_two[2 + px]
    total = got_two[0].astype(f32)
    for k in range(1, 6):
        total += got_two[k].astype(f32)
    down_two = total.astype(bf16)
    for c in x_far:
        c.wait()
    down_one = []
    for i in range(2):
        for j in range(2):
            value = field_one[i, j] + nt(down_two, ttwo[i, j])
            value += got_one[0, i, j].astype(f32) + got_one[1, i, j].astype(f32)
            part_one[0, i, j] = value.astype(bf16)

    def descend(n, c):
        i, h = n // 2, lax.rem(n, 2)
        for b in range(2):
            j = 2 * h + b
            value = field_zero[i, j] + nt(part_one[0, i // 2, h], tone[i, j])
            down_zero[i, j] = (value + got_zero[i, j].astype(f32)).astype(bf16)
        return c

    lax.fori_loop(0, 8, descend, 0)

    for c in x_samples[2:]:
        c.wait()
    for e in range(2):

        @pl.when(px != e)
        def _():
            near_edge(e)

    def store(i):
        return pltpu.make_async_copy(part_zero.at[i], out.at[i], out_sem.at[i])

    for i in (1, 2, 0, 3):
        for j in range(4):
            value = near_sum[i, j] + nt(basis[i, j], down_zero[i, j])
            if j in (0, 3):
                for sr in range(max(i - 1, 0), min(i + 1, 3) + 1):
                    value += nn(tiles[halo_tile[(i, j, sr)]], ext_s[sr, 5 * (j // 3)])
            if i in (1, 2):
                part_zero[i, j] = value.astype(bf16)
            else:
                near_sum[i, j] = value
        if i in (1, 2):
            store(i).start()
    for c in x_near:
        c.wait()
    for e in range(2):
        for j in range(4):
            part_zero[3 * e, j] = (near_sum[3 * e, j] + got_near[e, j].astype(f32)).astype(bf16)
        store(3 * e).start()
    for i in range(4):
        store(i).wait()


def solution(mesh):
    nx, ny = mesh.shape["qx"], mesh.shape["qy"]

    def per_device(
        positions,
        samples,
        leaf_basis,
        transfer_one,
        transfer_two,
        couplings,
        near_lists,
        far_zero,
        far_one,
        far_two,
    ):
        def body(*refs):
            kernel(4 * nx, 4 * ny, *refs)

        hbm = pl.BlockSpec(memory_space=pl.ANY)
        vmem = pl.BlockSpec(memory_space=pltpu.VMEM)
        block = (256, 256)
        return pl.pallas_call(
            body,
            out_shape=jax.ShapeDtypeStruct(samples.shape, bf16),
            in_specs=[hbm] * 6 + [vmem] * 4,
            out_specs=hbm,
            scratch_shapes=[
                pltpu.VMEM((4, 4) + block, bf16),
                pltpu.VMEM((4, 4) + block, bf16),
                pltpu.VMEM((2, 2) + block, bf16),
                pltpu.VMEM((3, 20) + block, bf16),
                pltpu.VMEM((36, 2, 256), f32),
                pltpu.VMEM((4, 6) + block, bf16),
                pltpu.VMEM((4, 8) + block, bf16),
                pltpu.VMEM((2, 6) + block, bf16),
                pltpu.VMEM((6,) + block, bf16),
                pltpu.VMEM((4, 4) + block, f32),
                pltpu.VMEM((2, 2) + block, f32),
                pltpu.VMEM((4, 4) + block, f32),
                pltpu.VMEM((4, 4) + block, bf16),
                pltpu.VMEM((4, 4) + block, bf16),
                pltpu.VMEM((2, 2, 2) + block, bf16),
                pltpu.VMEM((2, 2, 2) + block, bf16),
                pltpu.VMEM((6,) + block, bf16),
                pltpu.VMEM((6,) + block, bf16),
                pltpu.VMEM((2, 4) + block, bf16),
                pltpu.VMEM((2, 4) + block, bf16),
                pltpu.VMEM((8, 4, 48, 128), f32),
                pltpu.VMEM((6, 2, 48, 128), f32),
                pltpu.VMEM((6, 8, 128), f32),
                pltpu.VMEM((48, 128), f32),
                pltpu.VMEM((6, 4, 24, 128), f32),
                pltpu.VMEM((42,) + block, bf16),
                pltpu.VMEM((2, 2, 256, 128), f32),
                pltpu.VMEM((4, 4) + block, f32),
                pltpu.VMEM((2, 2) + block, f32),
                pltpu.VMEM((4, 4) + block, bf16),
                pltpu.SemaphoreType.DMA((13,)),
                pltpu.SemaphoreType.DMA((36,)),
                pltpu.SemaphoreType.DMA((4,)),
                pltpu.SemaphoreType.DMA((58,)),
                pltpu.SemaphoreType.DMA((58,)),
            ],
            compiler_params=pltpu.CompilerParams(
                collective_id=0, has_side_effects=True, vmem_limit_bytes=60 << 20
            ),
        )(
            positions,
            samples,
            leaf_basis,
            transfer_one,
            transfer_two,
            couplings,
            near_lists,
            far_zero,
            far_one,
            far_two,
        )

    cell = P("qx", "qy", None, None)
    short = P("qx", "qy", None)
    return jax.shard_map(
        per_device,
        mesh=mesh,
        in_specs=(P(), cell, cell, cell, cell, P(), short, short, short, short),
        out_specs=cell,
        check_vma=False,
    )
```

```python
import jax
import jax.numpy as jnp
from jax import lax
from jax.experimental import pallas as pl
from jax.experimental.pallas import tpu as pltpu
from jax.sharding import PartitionSpec as P

MESH = pl.DeviceIdType.MESH
bf16 = jnp.bfloat16
f32 = jnp.float32
LOG2E = 1.4426950408889634
LN2 = 0.6931471805599453
ROOT3 = 1.7320508075688772

HALF_INDEX = {}
for _u in range(0, 4):
    for _v in range(-3, 4):
        if max(abs(_u), abs(_v)) >= 2 and (_u > 0 or _v > 0):
            HALF_INDEX[(_u, _v)] = len(HALF_INDEX)


def nn(a, b):
    return jnp.dot(a, b, preferred_element_type=f32)


def nt(a, b):
    return lax.dot_general(a, b, (((1,), (1,)), ((), ())), preferred_element_type=f32)


def coupled(x, coup, level, u, v):
    if (u, v) in HALF_INDEX:
        return nt(x, coup[level, HALF_INDEX[(u, v)]])
    return nn(x, coup[level, HALF_INDEX[(-u, -v)]])


def far_pair(u, v):
    return max(abs(u), abs(v)) >= 2


def kernel(
    gx0,
    gy0,
    positions,
    samples,
    leaf_basis,
    transfer_one,
    transfer_two,
    couplings,
    near_lists,
    far_zero,
    far_one,
    far_two,
    out,
    basis,
    tone,
    ttwo,
    coup,
    pos,
    ext_s,
    ext_zero,
    ext_one,
    ext_two,
    field_zero,
    field_one,
    near_sum,
    part_zero,
    got_zero,
    part_one,
    got_one,
    part_two,
    got_two,
    part_near,
    got_near,
    mask_zero,
    mask_one,
    mask_two,
    own_two,
    mask_near,
    tiles,
    cols,
    half_zero,
    edge_near,
    down_zero,
    load_sem,
    pos_sem,
    out_sem,
    send,
    recv,
):
    X = lax.axis_index("qx")
    Y = lax.axis_index("qy")
    nx, ny = gx0 // 4, gy0 // 4
    px, py = lax.rem(X, 2), lax.rem(Y, 2)

    def at_x(k):
        return (lax.rem(X - px - 2 + k + nx, nx), Y)

    def at_y(k):
        return (X, lax.rem(Y - py - 2 + k + ny, ny))

    up, down = (lax.rem(X + nx - 1, nx), Y), (lax.rem(X + 1, nx), Y)
    left, right = (X, lax.rem(Y + ny - 1, ny)), (X, lax.rem(Y + 1, ny))

    def load(src, dst, n):
        return pltpu.make_async_copy(src, dst, load_sem.at[n])

    s_loads = [load(samples.at[r], ext_s.at[r, pl.ds(1, 4)], r) for r in range(4)]
    l_loads = [load(leaf_basis.at[r], basis.at[r], 4 + r) for r in range(4)]
    t_loads = [load(transfer_one, tone, 8), load(transfer_two, ttwo, 9)]
    c_loads = [load(couplings.at[l], coup.at[l], 10 + l) for l in range(3)]
    for r in range(4):
        s_loads[r].start()
        l_loads[r].start()

    def pos_copy(n):
        i, j = n // 6, lax.rem(n, 6)
        row = lax.rem(4 * X - 1 + i + gx0, gx0)
        col = lax.rem(4 * Y - 1 + j + gy0, gy0)
        return pltpu.make_async_copy(positions.at[row, col], pos.at[n], pos_sem.at[n])

    def start_pos(n, c):
        pos_copy(n).start()
        return c

    barrier = pltpu.get_barrier_semaphore()
    for k in range(6):

        @pl.when(k != 2 + px)
        def _():
            pl.semaphore_signal(barrier, inc=1, device_id=at_x(k), device_id_type=MESH)

        @pl.when(k != 2 + py)
        def _():
            pl.semaphore_signal(barrier, inc=1, device_id=at_y(k), device_id_type=MESH)

    for c in t_loads + c_loads:
        c.start()
    lax.fori_loop(0, 36, start_pos, 0)

    def mask_of(lst, row0, col0, rows, grid_rows, grid_cols, width):
        k = lax.broadcasted_iota(jnp.int32, (rows, 1), 0)
        b = k & 7
        r, c = row0 + (k >> 3), col0 + b
        ok = (r >= 0) & (r < grid_rows) & (c >= 0) & (c < grid_cols) & (b < width)
        ident = jnp.where(ok, r * grid_cols + c, -2)
        hit = jnp.max(jnp.where(ident == lst, 1.0, 0.0), axis=1, keepdims=True)
        return jnp.broadcast_to(hit, (rows, 128))

    for i in range(4):
        for j in range(4):
            r0, c0 = 4 * X + 2 * (i // 2) - 2, 4 * Y + 2 * (j // 2) - 2
            mask_zero[i + 2, j] = mask_of(far_zero[i, j : j + 1, :], r0, c0, 48, gx0, gy0, 6)
            mask_near[i + 1, j] = mask_of(
                near_lists[i, j : j + 1, :], 4 * X + i - 1, 4 * Y + j - 1, 24, gx0, gy0, 3
            )
    for i in range(2):
        for j in range(2):
            mask_one[i + 2, j] = mask_of(
                far_one[i, j : j + 1, :], 2 * X - 2, 2 * Y - 2, 48, gx0 // 2, gy0 // 2, 6
            )
    own_two[...] = mask_of(
        far_two[0, 0:1, :], X - px - 2, Y - py - 2, 48, gx0 // 4, gy0 // 4, 6
    )

    pl.semaphore_wait(barrier, 10)

    def remote(src, dst, n, dev):
        return pltpu.make_async_remote_copy(
            src_ref=src,
            dst_ref=dst,
            send_sem=send.at[n],
            recv_sem=recv.at[n],
            device_id=dev,
            device_id_type=MESH,
        )

    x_samples = []
    for half in range(2):
        rows = pl.ds(2 * px if half == 0 else 2 - 2 * px, 2)
        x_samples += [
            remote(samples.at[rows, 3], ext_s.at[rows, 0], 30 * half, right),
            remote(samples.at[rows, 0], ext_s.at[rows, 5], 30 * half + 1, left),
        ]
    x_samples[0].start()
    x_samples[1].start()
    rows_lo, rows_hi = pl.ds(0, 16), pl.ds(32, 16)
    x_masks = [
        remote(mask_zero.at[pl.ds(4, 2), :, rows_hi], mask_zero.at[pl.ds(0, 2), :, rows_hi], 2, down),
        remote(mask_zero.at[pl.ds(2, 2), :, rows_lo], mask_zero.at[pl.ds(6, 2), :, rows_lo], 3, up),
        remote(mask_one.at[pl.ds(2, 2), :, rows_hi], mask_one.at[pl.ds(0, 2), :, rows_hi], 4, down),
        remote(mask_one.at[pl.ds(2, 2), :, rows_lo], mask_one.at[pl.ds(4, 2), :, rows_lo], 5, up),
        remote(mask_near.at[4, :, pl.ds(16, 8)], mask_near.at[0, :, pl.ds(16, 8)], 6, down),
        remote(mask_near.at[1, :, pl.ds(0, 8)], mask_near.at[5, :, pl.ds(0, 8)], 7, up),
    ]
    for c in x_masks:
        c.start()

    def x_mask_two(k):
        slot = px + 4 - 2 * (k // 2)
        return pltpu.make_async_remote_copy(
            src_ref=own_two.at[pl.ds(8 * k, 8)],
            dst_ref=mask_two.at[slot],
            send_sem=send.at[40 + k],
            recv_sem=recv.at[40 + slot],
            device_id=at_x(k),
            device_id_type=MESH,
        )

    def x_two(k):
        source, slot, dev = (
            (2 + py, 2 - py, right),
            (2 + py, 4 - py, left),
            (1 + py, 1 - py, right),
            (3 + py, 5 - py, left),
            (5 * py, 5 * py, (X, Y + 1 - 2 * py)),
        )[k]
        return pltpu.make_async_remote_copy(
            src_ref=ext_two.at[source],
            dst_ref=ext_two.at[slot],
            send_sem=send.at[46 + k],
            recv_sem=recv.at[46 + slot],
            device_id=dev,
            device_id_type=MESH,
        )

    def x_part_two(k):
        slot = px + 4 - 2 * (k // 2)
        return pltpu.make_async_remote_copy(
            src_ref=part_two.at[k],
            dst_ref=got_two.at[slot],
            send_sem=send.at[52 + k],
            recv_sem=recv.at[52 + slot],
            device_id=at_x(k),
            device_id_type=MESH,
        )

    def recv_wait(dst, n):
        pltpu.make_async_copy(dst, dst, recv.at[n]).wait()

    for k in range(6):

        @pl.when(k != 2 + px)
        def _():
            x_mask_two(k).start()

    mask_two[2 + px] = own_two[pl.ds(pl.multiple_of(8 * (2 + px), 8), 8), :]

    x_zero = []
    for r in range(4):
        s_loads[r].wait()
        l_loads[r].wait()
        for j in range(4):
            ext_zero[r, 2 + j] = nn(ext_s[r, 1 + j].T, basis[r, j]).astype(bf16)
    for q in range(4):
        r = lax.rem(q + 2 * px, 4)
        x_zero += [
            remote(ext_zero.at[r, pl.ds(4, 2)], ext_zero.at[r, pl.ds(0, 2)], 8 + 2 * q, right),
            remote(ext_zero.at[r, pl.ds(2, 2)], ext_zero.at[r, pl.ds(6, 2)], 9 + 2 * q, left),
        ]

    t_loads[0].wait()
    x_one = []
    for i in range(2):
        for j in range(2):
            total = None
            for a in range(2):
                for b in range(2):
                    term = nn(ext_zero[2 * i + a, 2 + 2 * j + b], tone[2 * i + a, 2 * j + b])
                    total = term if total is None else total + term
            ext_one[i, 2 + j] = total.astype(bf16)
        x_one.append(remote(ext_one.at[i, pl.ds(2, 2)], ext_one.at[i, pl.ds(0, 2)], 16 + 2 * i, right))
        x_one.append(remote(ext_one.at[i, pl.ds(2, 2)], ext_one.at[i, pl.ds(4, 2)], 17 + 2 * i, left))

    t_loads[1].wait()
    total = None
    for a in range(2):
        for b in range(2):
            term = nn(ext_one[a, 2 + b], ttwo[a, b])
            total = term if total is None else total + term
    ext_two[2 + py] = total.astype(bf16)
    x_two(0).start()
    x_two(1).start()
    x_zero[0].start()
    x_zero[1].start()

    def wait_pos(n, c):
        pos_copy(n).wait()
        return c

    lax.fori_loop(0, 36, wait_pos, 0)
    pos[...] = pos[...] * (ROOT3 * LOG2E)

    for c in x_masks:
        c.wait()
    c_loads[0].wait()

    def zero_rows(i):
        if i < 0:
            return (0, 1), 4
        if i > 3:
            return (2, 3), -2
        return (0, 1, 2, 3), (2 if i < 2 else 0)

    def zero_terms(i, j, halo):
        rows, shift = zero_rows(i)
        for sr in rows:
            for b in range(6):
                column = 2 * (j // 2) + b
                u, v = sr - i, b - 2 - j % 2
                if far_pair(u, v) and halo == (not 2 <= column < 6):
                    yield sr, column, u, v, (sr + shift) * 8 + b

    def zero_term(i, j, sr, column, u, v, row):
        m = mask_zero[i + 2, j, pl.ds(row, 1), :]
        m = jnp.concatenate([m, m], axis=1).astype(bf16)
        return coupled(ext_zero[sr, column] * m, coup, 0, u, v)

    def zero_work(targets):
        for i, j in targets:
            total = None
            for term in zero_terms(i, j, False):
                if total is not None:
                    yield True
                value = zero_term(i, j, *term)
                total = value if total is None else total + value
            if 0 <= i < 4:
                field_zero[i, j] = total
            else:
                half_zero[i + 2 if i < 0 else i - 2, j] = total
            yield False

    halo_tile = {}

    def near_sources(i, j):
        for sr in range(max(i - 1, 0), min(i + 1, 3) + 1):
            for b in range(3):
                yield sr, j + b

    jobs = [(i, j) for i in (-1, 4, 0, 1, 2, 3) for j in range(4)]

    def make_tile(target, slot, i, j, sr, column, spans):
        there = pos[(sr + 1) * 6 + column]
        xs, ys = there[0:1], there[1:2]
        mask = mask_near[i + 1, j, pl.ds((sr - i + 1) * 8 + column - j, 1), :]
        c0, c1 = mask * 0.0625, mask * (0.0625 * LN2)
        for h in range(2):
            lanes = slice(128 * h, 128 * h + 128)
            for span in spans:
                dx = cols[target, 0, span, :] - xs[:, lanes]
                dy = cols[target, 1, span, :] - ys[:, lanes]
                d2 = jnp.maximum(dx * dx + dy * dy, 1e-30)
                d = d2 * lax.rsqrt(d2)
                value = (c0 + c1 * d) * jnp.exp2(-d)
                tiles[slot, span, lanes] = value.astype(bf16)

    def near_work(i, j, terms):
        total = None
        for slot, sr, column in terms:
            value = nn(tiles[slot], ext_s[sr, column])
            total = value if total is None else total + value
            yield
        if 0 <= i < 4:
            near_sum[i, j] = total
        elif j in (1, 2):
            part_near[0 if i < 0 else 1, j] = total.astype(bf16)
        else:
            edge_near[0 if i < 0 else 1, j // 2] = total

    def level_two():
        c_loads[2].wait()
        for k in range(5):
            x_two(k).wait_send()
        recv_wait(ext_two.at[5 - 5 * py], 51 - 5 * py)
        for k in range(6):

            @pl.when(k != 2 + px)
            def _():
                x_mask_two(k).wait_send()
                recv_wait(mask_two.at[k], 40 + k)

        for qy in range(2):
            for u in range(-3, 4):
                k = px + 2 - u

                @pl.when((py == qy) & (k >= 0) & (k < 6))
                def _():
                    total = None
                    for b in range(6):
                        v = b - 2 - qy
                        if not far_pair(u, v):
                            continue
                        m = mask_two[k, pl.ds(b, 1), :]
                        m = jnp.concatenate([m, m], axis=1).astype(bf16)
                        term = coupled(ext_two[b] * m, coup, 2, u, v)
                        total = term if total is None else total + term
                    part_two[k] = total.astype(bf16)

        for k in range(6):

            @pl.when(k != 2 + px)
            def _():
                x_part_two(k).start()

    def halo_row(i):
        for j in range(4):
            if i < 0:
                total = half_zero[i + 2, j]
            elif i > 3:
                total = half_zero[i - 2, j]
            else:
                total = field_zero[i, j]
            for term in zero_terms(i, j, True):
                total += zero_term(i, j, *term)
            if i < 0:
                part_zero[i + 2, j] = total.astype(bf16)
            elif i > 3:
                part_zero[i - 2, j] = total.astype(bf16)
            else:
                field_zero[i, j] = total

    x_far = [
        remote(part_zero.at[pl.ds(0, 2)], got_zero.at[pl.ds(2, 2)], 22, up),
        remote(part_zero.at[pl.ds(2, 2)], got_zero.at[pl.ds(0, 2)], 23, down),
    ]

    def far_edge(e):
        for i in ((-2, -1), (4, 5))[e]:
            halo_row(i)
        x_far[e].start()

    x_near = [
        remote(part_near.at[0], got_near.at[1], 20, up),
        remote(part_near.at[1], got_near.at[0], 21, down),
    ]

    def near_edge(e):
        for side in range(2):
            j, column = 3 * side, 5 * side
            value = nn(tiles[halo_tile[(5 * e - 1, j, 3 * e)]], ext_s[3 * e, column])
            part_near[e, j] = (edge_near[e, side] + value).astype(bf16)
        x_near[e].start()

    far_order = [(i, j) for i in (-2, -1, 4, 5, 0, 1, 2, 3) for j in range(4)]
    count = sum(1 for i, j in jobs if i in (1, 2) for _ in near_sources(i, j))
    rate = sum(1 for i, j in far_order for _ in zero_terms(i, j, False)) / count
    far, before, owed = zero_work(far_order), iter(()), 0.0
    for n, (i, j) in enumerate(jobs):
        here = pos[(i + 1) * 6 + j + 1]
        cols[n % 2, 0] = jnp.broadcast_to(here[0:1], (128, 256)).T
        cols[n % 2, 1] = jnp.broadcast_to(here[1:2], (128, 256)).T
        terms, made = [], []
        for q, (sr, column) in enumerate(near_sources(i, j)):
            if 1 <= column < 5:
                slot = 9 * (n % 2) + q
                terms.append((slot, sr, column))
            else:
                slot = 18 + len(halo_tile)
                halo_tile[(i, j, sr)] = slot
            made.append((n % 2, slot, i, j, sr, column))
            if i in (-1, 0, 3, 4):
                continue
            make_tile(*made[-1], [pl.ds(64 * w, 64) for w in range(4)])
            owed += rate
            while owed >= 1.0:
                next(far, None)
                owed -= 1.0
            next(before, None)
        for _ in before:
            pass
        if i in (-1, 0, 3, 4):
            while next(far, False) if n > 19 else False:
                pass

            def chunk(w, c):
                for item in made:
                    make_tile(*item, [pl.ds(pl.multiple_of(64 * w, 64), 64)])
                return c

            lax.fori_loop(0, 4, chunk, 0)
        before = near_work(i, j, terms)
        if n == 4:
            recv_wait(ext_two.at[1 + py], 47 + py)
            recv_wait(ext_two.at[3 + py], 49 + py)
            x_two(2).start()
            x_two(3).start()
            x_zero[2].start()
            x_zero[3].start()
        if n == 11:
            recv_wait(ext_two.at[py], 46 + py)
            recv_wait(ext_two.at[4 + py], 50 + py)
            x_two(4).start()
            for c in x_one + x_zero[4:] + x_samples[2:]:
                c.start()
        if n in (13, 16):
            while next(far, False):
                owed -= 1.0
        if n == 13:
            level_two()
            for c in x_samples[:2]:
                c.wait()
            for e in range(2):

                @pl.when(px == e)
                def _():
                    near_edge(e)

        if n == 16:
            for c in x_zero[:4]:
                c.wait()
            for e in range(2):

                @pl.when(px == e)
                def _():
                    far_edge(e)

    for _ in before:
        pass
    for _ in far:
        pass

    c_loads[1].wait()
    for c in x_one:
        c.wait()

    def far_one_row(i):
        for j in range(2):
            total = None
            for sr in range(2):
                for b in range(6):
                    u, v = sr - i, b - 2 - j
                    if not far_pair(u, v):
                        continue
                    a = sr + 2 if 0 <= i < 2 else (sr + 4 if i < 0 else sr)
                    m = mask_one[i + 2, j, pl.ds(a * 8 + b, 1), :]
                    m = jnp.concatenate([m, m], axis=1).astype(bf16)
                    term = coupled(ext_one[sr, b] * m, coup, 1, u, v)
                    total = term if total is None else total + term
            if i < 0:
                part_one[0, i + 2, j] = total.astype(bf16)
            elif i > 1:
                part_one[1, i - 2, j] = total.astype(bf16)
            else:
                field_one[i, j] = total

    far_one_row(-2)
    far_one_row(-1)
    x_far.append(remote(part_one.at[0], got_one.at[1], 24, up))
    x_far[2].start()
    far_one_row(2)
    far_one_row(3)
    x_far.append(remote(part_one.at[1], got_one.at[0], 25, down))
    x_far[3].start()

    far_one_row(0)
    far_one_row(1)

    for k in range(6):

        @pl.when(k != 2 + px)
        def _():
            x_part_two(k).wait_send()
            recv_wait(got_two.at[k], 52 + k)

    got_two[2 + px] = part_two[2 + px]
    total = got_two[0].astype(f32)
    for k in range(1, 6):
        total += got_two[k].astype(f32)
    down_two = total.astype(bf16)
    for c in x_far[2:]:
        c.wait()
    down_one = []
    for i in range(2):
        for j in range(2):
            value = field_one[i, j] + nt(down_two, ttwo[i, j])
            value += got_one[0, i, j].astype(f32) + got_one[1, i, j].astype(f32)
            part_one[0, i, j] = value.astype(bf16)

    for c in x_zero[4:]:
        c.wait()
    for e in range(2):

        @pl.when(px != e)
        def _():
            far_edge(e)

    for i in range(4):
        halo_row(i)

    for c in x_far[:2]:
        c.wait()

    def descend(n, c):
        i, h = n // 2, lax.rem(n, 2)
        for b in range(2):
            j = 2 * h + b
            value = field_zero[i, j] + nt(part_one[0, i // 2, h], tone[i, j])
            down_zero[i, j] = (value + got_zero[i, j].astype(f32)).astype(bf16)
        return c

    lax.fori_loop(0, 8, descend, 0)

    for c in x_samples[2:]:
        c.wait()
    for e in range(2):

        @pl.when(px != e)
        def _():
            near_edge(e)

    def store(i):
        return pltpu.make_async_copy(near_sum.at[i], out.at[i], out_sem.at[i])

    for i in (1, 2, 0, 3):
        for j in range(4):
            value = near_sum[i, j] + nt(basis[i, j], down_zero[i, j])
            if j in (0, 3):
                for sr in range(max(i - 1, 0), min(i + 1, 3) + 1):
                    value += nn(tiles[halo_tile[(i, j, sr)]], ext_s[sr, 5 * (j // 3)])
            near_sum[i, j] = value
        if i in (1, 2):
            store(i).start()
    for c in x_near:
        c.wait()
    for e in range(2):
        for j in range(4):
            near_sum[3 * e, j] += got_near[e, j].astype(f32)
        store(3 * e).start()
    for i in range(4):
        store(i).wait()


def solution(mesh):
    nx, ny = mesh.shape["qx"], mesh.shape["qy"]

    def per_device(
        positions,
        samples,
        leaf_basis,
        transfer_one,
        transfer_two,
        couplings,
        near_lists,
        far_zero,
        far_one,
        far_two,
    ):
        def body(*refs):
            kernel(4 * nx, 4 * ny, *refs)

        hbm = pl.BlockSpec(memory_space=pl.ANY)
        vmem = pl.BlockSpec(memory_space=pltpu.VMEM)
        block = (256, 256)
        return pl.pallas_call(
            body,
            out_shape=jax.ShapeDtypeStruct(samples.shape, f32),
            in_specs=[hbm] * 6 + [vmem] * 4,
            out_specs=hbm,
            scratch_shapes=[
                pltpu.VMEM((4, 4) + block, bf16),
                pltpu.VMEM((4, 4) + block, bf16),
                pltpu.VMEM((2, 2) + block, bf16),
                pltpu.VMEM((3, 20) + block, bf16),
                pltpu.VMEM((36, 2, 256), f32),
                pltpu.VMEM((4, 6) + block, bf16),
                pltpu.VMEM((4, 8) + block, bf16),
                pltpu.VMEM((2, 6) + block, bf16),
                pltpu.VMEM((6,) + block, bf16),
                pltpu.VMEM((4, 4) + block, f32),
                pltpu.VMEM((2, 2) + block, f32),
                pltpu.VMEM((4, 4) + block, f32),
                pltpu.VMEM((4, 4) + block, bf16),
                pltpu.VMEM((4, 4) + block, bf16),
                pltpu.VMEM((2, 2, 2) + block, bf16),
                pltpu.VMEM((2, 2, 2) + block, bf16),
                pltpu.VMEM((6,) + block, bf16),
                pltpu.VMEM((6,) + block, bf16),
                pltpu.VMEM((2, 4) + block, bf16),
                pltpu.VMEM((2, 4) + block, bf16),
                pltpu.VMEM((8, 4, 48, 128), f32),
                pltpu.VMEM((6, 2, 48, 128), f32),
                pltpu.VMEM((6, 8, 128), f32),
                pltpu.VMEM((48, 128), f32),
                pltpu.VMEM((6, 4, 24, 128), f32),
                pltpu.VMEM((42,) + block, bf16),
                pltpu.VMEM((2, 2, 256, 128), f32),
                pltpu.VMEM((4, 4) + block, f32),
                pltpu.VMEM((2, 2) + block, f32),
                pltpu.VMEM((4, 4) + block, bf16),
                pltpu.SemaphoreType.DMA((13,)),
                pltpu.SemaphoreType.DMA((36,)),
                pltpu.SemaphoreType.DMA((4,)),
                pltpu.SemaphoreType.DMA((58,)),
                pltpu.SemaphoreType.DMA((58,)),
            ],
            compiler_params=pltpu.CompilerParams(
                collective_id=0, has_side_effects=True, vmem_limit_bytes=60 << 20
            ),
        )(
            positions,
            samples,
            leaf_basis,
            transfer_one,
            transfer_two,
            couplings,
            near_lists,
            far_zero,
            far_one,
            far_two,
        ).astype(bf16)

    cell = P("qx", "qy", None, None)
    short = P("qx", "qy", None)
    return jax.shard_map(
        per_device,
        mesh=mesh,
        in_specs=(P(), cell, cell, cell, cell, P(), short, short, short, short),
        out_specs=cell,
        check_vma=False,
    )
```

```python
import jax
import jax.numpy as jnp
from jax import lax
from jax.experimental import pallas as pl
from jax.experimental.pallas import tpu as pltpu
from jax.sharding import PartitionSpec as P

MESH = pl.DeviceIdType.MESH
bf16 = jnp.bfloat16
f32 = jnp.float32
LOG2E = 1.4426950408889634
LN2 = 0.6931471805599453
ROOT3 = 1.7320508075688772

HALF_INDEX = {}
for _u in range(0, 4):
    for _v in range(-3, 4):
        if max(abs(_u), abs(_v)) >= 2 and (_u > 0 or _v > 0):
            HALF_INDEX[(_u, _v)] = len(HALF_INDEX)


def nn(a, b):
    return jnp.dot(a, b, preferred_element_type=f32)


def nt(a, b):
    return lax.dot_general(a, b, (((1,), (1,)), ((), ())), preferred_element_type=f32)


def coupled(x, coup, level, u, v):
    if (u, v) in HALF_INDEX:
        return nt(x, coup[level, HALF_INDEX[(u, v)]])
    return nn(x, coup[level, HALF_INDEX[(-u, -v)]])


def far_pair(u, v):
    return max(abs(u), abs(v)) >= 2


def kernel(
    gx0,
    gy0,
    positions,
    samples,
    leaf_basis,
    transfer_one,
    transfer_two,
    couplings,
    near_lists,
    far_zero,
    far_one,
    far_two,
    out,
    basis,
    tone,
    ttwo,
    coup,
    pos,
    ext_s,
    ext_zero,
    ext_one,
    ext_two,
    field_zero,
    field_one,
    near_sum,
    part_zero,
    got_zero,
    part_one,
    got_one,
    part_two,
    got_two,
    part_near,
    got_near,
    mask_zero,
    mask_one,
    mask_two,
    own_two,
    mask_near,
    tiles,
    cols,
    half_zero,
    edge_near,
    down_zero,
    load_sem,
    pos_sem,
    out_sem,
    send,
    recv,
):
    X = lax.axis_index("qx")
    Y = lax.axis_index("qy")
    nx, ny = gx0 // 4, gy0 // 4
    px, py = lax.rem(X, 2), lax.rem(Y, 2)

    def at_x(k):
        return (lax.rem(X - px - 2 + k + nx, nx), Y)

    def at_y(k):
        return (X, lax.rem(Y - py - 2 + k + ny, ny))

    up, down = (lax.rem(X + nx - 1, nx), Y), (lax.rem(X + 1, nx), Y)
    left, right = (X, lax.rem(Y + ny - 1, ny)), (X, lax.rem(Y + 1, ny))

    def load(src, dst, n):
        return pltpu.make_async_copy(src, dst, load_sem.at[n])

    s_loads = [load(samples.at[r], ext_s.at[r, pl.ds(1, 4)], r) for r in range(4)]
    l_loads = [load(leaf_basis.at[r], basis.at[r], 4 + r) for r in range(4)]
    t_loads = [load(transfer_one, tone, 8), load(transfer_two, ttwo, 9)]
    c_loads = [load(couplings.at[l], coup.at[l], 10 + l) for l in range(3)]
    for r in range(4):
        s_loads[r].start()
        l_loads[r].start()

    def pos_copy(n):
        i, j = n // 6, lax.rem(n, 6)
        row = lax.rem(4 * X - 1 + i + gx0, gx0)
        col = lax.rem(4 * Y - 1 + j + gy0, gy0)
        return pltpu.make_async_copy(positions.at[row, col], pos.at[n], pos_sem.at[n])

    def start_pos(n, c):
        pos_copy(n).start()
        return c

    barrier = pltpu.get_barrier_semaphore()
    for k in range(6):

        @pl.when(k != 2 + px)
        def _():
            pl.semaphore_signal(barrier, inc=1, device_id=at_x(k), device_id_type=MESH)

        @pl.when(k != 2 + py)
        def _():
            pl.semaphore_signal(barrier, inc=1, device_id=at_y(k), device_id_type=MESH)

    for c in t_loads + c_loads:
        c.start()
    lax.fori_loop(0, 36, start_pos, 0)

    def mask_of(lst, row0, col0, rows, grid_rows, grid_cols, width):
        k = lax.broadcasted_iota(jnp.int32, (rows, 1), 0)
        b = k & 7
        r, c = row0 + (k >> 3), col0 + b
        ok = (r >= 0) & (r < grid_rows) & (c >= 0) & (c < grid_cols) & (b < width)
        ident = jnp.where(ok, r * grid_cols + c, -2)
        hit = jnp.max(jnp.where(ident == lst, 1.0, 0.0), axis=1, keepdims=True)
        return jnp.broadcast_to(hit, (rows, 128))

    for i in range(4):
        for j in range(4):
            r0, c0 = 4 * X + 2 * (i // 2) - 2, 4 * Y + 2 * (j // 2) - 2
            mask_zero[i + 2, j] = mask_of(far_zero[i, j : j + 1, :], r0, c0, 48, gx0, gy0, 6)
            mask_near[i + 1, j] = mask_of(
                near_lists[i, j : j + 1, :], 4 * X + i - 1, 4 * Y + j - 1, 24, gx0, gy0, 3
            )
    for i in range(2):
        for j in range(2):
            mask_one[i + 2, j] = mask_of(
                far_one[i, j : j + 1, :], 2 * X - 2, 2 * Y - 2, 48, gx0 // 2, gy0 // 2, 6
            )
    own_two[...] = mask_of(
        far_two[0, 0:1, :], X - px - 2, Y - py - 2, 48, gx0 // 4, gy0 // 4, 6
    )

    pl.semaphore_wait(barrier, 10)

    def remote(src, dst, n, dev):
        return pltpu.make_async_remote_copy(
            src_ref=src,
            dst_ref=dst,
            send_sem=send.at[n],
            recv_sem=recv.at[n],
            device_id=dev,
            device_id_type=MESH,
        )

    x_samples = []
    for half in range(2):
        rows = pl.ds(2 * px if half == 0 else 2 - 2 * px, 2)
        x_samples += [
            remote(samples.at[rows, 3], ext_s.at[rows, 0], 30 * half, right),
            remote(samples.at[rows, 0], ext_s.at[rows, 5], 30 * half + 1, left),
        ]
    x_samples[0].start()
    x_samples[1].start()
    rows_lo, rows_hi = pl.ds(0, 16), pl.ds(32, 16)
    x_masks = [
        remote(mask_zero.at[pl.ds(4, 2), :, rows_hi], mask_zero.at[pl.ds(0, 2), :, rows_hi], 2, down),
        remote(mask_zero.at[pl.ds(2, 2), :, rows_lo], mask_zero.at[pl.ds(6, 2), :, rows_lo], 3, up),
        remote(mask_one.at[pl.ds(2, 2), :, rows_hi], mask_one.at[pl.ds(0, 2), :, rows_hi], 4, down),
        remote(mask_one.at[pl.ds(2, 2), :, rows_lo], mask_one.at[pl.ds(4, 2), :, rows_lo], 5, up),
        remote(mask_near.at[4, :, pl.ds(16, 8)], mask_near.at[0, :, pl.ds(16, 8)], 6, down),
        remote(mask_near.at[1, :, pl.ds(0, 8)], mask_near.at[5, :, pl.ds(0, 8)], 7, up),
    ]
    for c in x_masks:
        c.start()

    def x_mask_two(k):
        slot = px + 4 - 2 * (k // 2)
        return pltpu.make_async_remote_copy(
            src_ref=own_two.at[pl.ds(8 * k, 8)],
            dst_ref=mask_two.at[slot],
            send_sem=send.at[40 + k],
            recv_sem=recv.at[40 + slot],
            device_id=at_x(k),
            device_id_type=MESH,
        )

    def x_two(k):
        source, slot, dev = (
            (2 + py, 2 - py, right),
            (2 + py, 4 - py, left),
            (1 + py, 1 - py, right),
            (3 + py, 5 - py, left),
            (5 * py, 5 * py, (X, Y + 1 - 2 * py)),
        )[k]
        return pltpu.make_async_remote_copy(
            src_ref=ext_two.at[source],
            dst_ref=ext_two.at[slot],
            send_sem=send.at[46 + k],
            recv_sem=recv.at[46 + slot],
            device_id=dev,
            device_id_type=MESH,
        )

    def x_part_two(k):
        slot = px + 4 - 2 * (k // 2)
        return pltpu.make_async_remote_copy(
            src_ref=part_two.at[k],
            dst_ref=got_two.at[slot],
            send_sem=send.at[52 + k],
            recv_sem=recv.at[52 + slot],
            device_id=at_x(k),
            device_id_type=MESH,
        )

    def recv_wait(dst, n):
        pltpu.make_async_copy(dst, dst, recv.at[n]).wait()

    for k in range(6):

        @pl.when(k != 2 + px)
        def _():
            x_mask_two(k).start()

    mask_two[2 + px] = own_two[pl.ds(pl.multiple_of(8 * (2 + px), 8), 8), :]

    x_zero = []
    for r in range(4):
        s_loads[r].wait()
        l_loads[r].wait()
        for j in range(4):
            ext_zero[r, 2 + j] = nn(ext_s[r, 1 + j].T, basis[r, j]).astype(bf16)
    for q in range(4):
        r = lax.rem(q + 2 * px, 4)
        x_zero += [
            remote(ext_zero.at[r, pl.ds(4, 2)], ext_zero.at[r, pl.ds(0, 2)], 8 + 2 * q, right),
            remote(ext_zero.at[r, pl.ds(2, 2)], ext_zero.at[r, pl.ds(6, 2)], 9 + 2 * q, left),
        ]

    t_loads[0].wait()
    x_one = []
    for i in range(2):
        for j in range(2):
            total = None
            for a in range(2):
                for b in range(2):
                    term = nn(ext_zero[2 * i + a, 2 + 2 * j + b], tone[2 * i + a, 2 * j + b])
                    total = term if total is None else total + term
            ext_one[i, 2 + j] = total.astype(bf16)
        x_one.append(remote(ext_one.at[i, pl.ds(2, 2)], ext_one.at[i, pl.ds(0, 2)], 16 + 2 * i, right))
        x_one.append(remote(ext_one.at[i, pl.ds(2, 2)], ext_one.at[i, pl.ds(4, 2)], 17 + 2 * i, left))

    t_loads[1].wait()
    total = None
    for a in range(2):
        for b in range(2):
            term = nn(ext_one[a, 2 + b], ttwo[a, b])
            total = term if total is None else total + term
    ext_two[2 + py] = total.astype(bf16)
    x_two(0).start()
    x_two(1).start()
    x_zero[0].start()
    x_zero[1].start()

    def wait_pos(n, c):
        pos_copy(n).wait()
        return c

    lax.fori_loop(0, 36, wait_pos, 0)
    pos[...] = pos[...] * (ROOT3 * LOG2E)

    for c in x_masks:
        c.wait()
    c_loads[0].wait()

    def zero_rows(i):
        if i < 0:
            return (0, 1), 4
        if i > 3:
            return (2, 3), -2
        return (0, 1, 2, 3), (2 if i < 2 else 0)

    def zero_terms(i, j, halo):
        rows, shift = zero_rows(i)
        for sr in rows:
            for b in range(6):
                column = 2 * (j // 2) + b
                u, v = sr - i, b - 2 - j % 2
                if far_pair(u, v) and halo == (not 2 <= column < 6):
                    yield sr, column, u, v, (sr + shift) * 8 + b

    def zero_term(i, j, sr, column, u, v, row):
        m = mask_zero[i + 2, j, pl.ds(row, 1), :]
        m = jnp.concatenate([m, m], axis=1).astype(bf16)
        return coupled(ext_zero[sr, column] * m, coup, 0, u, v)

    def zero_work(targets):
        for i, j in targets:
            total = None
            for term in zero_terms(i, j, False):
                if total is not None:
                    yield True
                value = zero_term(i, j, *term)
                total = value if total is None else total + value
            if 0 <= i < 4:
                field_zero[i, j] = total
            else:
                half_zero[i + 2 if i < 0 else i - 2, j] = total
            yield False

    halo_tile = {}

    def near_sources(i, j):
        for sr in range(max(i - 1, 0), min(i + 1, 3) + 1):
            for b in range(3):
                yield sr, j + b

    jobs = [(i, j) for i in (-1, 4, 0, 1, 2, 3) for j in range(4)]

    def make_tile(target, slot, i, j, sr, column):
        there = pos[(sr + 1) * 6 + column]
        xs, ys = there[0:1], there[1:2]
        mask = mask_near[i + 1, j, pl.ds((sr - i + 1) * 8 + column - j, 1), :]
        c0, c1 = mask * 0.0625, mask * (0.0625 * LN2)
        for h in range(2):
            lanes = slice(128 * h, 128 * h + 128)
            for w in range(4):
                span = slice(64 * w, 64 * w + 64)
                dx = cols[target, 0, span, :] - xs[:, lanes]
                dy = cols[target, 1, span, :] - ys[:, lanes]
                d2 = jnp.maximum(dx * dx + dy * dy, 1e-30)
                d = d2 * lax.rsqrt(d2)
                value = (c0 + c1 * d) * jnp.exp2(-d)
                tiles[slot, span, lanes] = value.astype(bf16)

    def near_work(i, j, terms):
        total = None
        for slot, sr, column in terms:
            value = nn(tiles[slot], ext_s[sr, column])
            total = value if total is None else total + value
            yield
        if 0 <= i < 4:
            near_sum[i, j] = total
        elif j in (1, 2):
            part_near[0 if i < 0 else 1, j] = total.astype(bf16)
        else:
            edge_near[0 if i < 0 else 1, j // 2] = total

    def level_two():
        c_loads[2].wait()
        for k in range(5):
            x_two(k).wait_send()
        recv_wait(ext_two.at[5 - 5 * py], 51 - 5 * py)
        for k in range(6):

            @pl.when(k != 2 + px)
            def _():
                x_mask_two(k).wait_send()
                recv_wait(mask_two.at[k], 40 + k)

        for qy in range(2):
            for u in range(-3, 4):
                k = px + 2 - u

                @pl.when((py == qy) & (k >= 0) & (k < 6))
                def _():
                    total = None
                    for b in range(6):
                        v = b - 2 - qy
                        if not far_pair(u, v):
                            continue
                        m = mask_two[k, pl.ds(b, 1), :]
                        m = jnp.concatenate([m, m], axis=1).astype(bf16)
                        term = coupled(ext_two[b] * m, coup, 2, u, v)
                        total = term if total is None else total + term
                    part_two[k] = total.astype(bf16)

        for k in range(6):

            @pl.when(k != 2 + px)
            def _():
                x_part_two(k).start()

    def halo_row(i):
        for j in range(4):
            if i < 0:
                total = half_zero[i + 2, j]
            elif i > 3:
                total = half_zero[i - 2, j]
            else:
                total = field_zero[i, j]
            for term in zero_terms(i, j, True):
                total += zero_term(i, j, *term)
            if i < 0:
                part_zero[i + 2, j] = total.astype(bf16)
            elif i > 3:
                part_zero[i - 2, j] = total.astype(bf16)
            else:
                field_zero[i, j] = total

    x_far = [
        remote(part_zero.at[pl.ds(0, 2)], got_zero.at[pl.ds(2, 2)], 22, up),
        remote(part_zero.at[pl.ds(2, 2)], got_zero.at[pl.ds(0, 2)], 23, down),
    ]

    def far_edge(e):
        for i in ((-2, -1), (4, 5))[e]:
            halo_row(i)
        x_far[e].start()

    x_near = [
        remote(part_near.at[0], got_near.at[1], 20, up),
        remote(part_near.at[1], got_near.at[0], 21, down),
    ]

    def near_edge(e):
        for side in range(2):
            j, column = 3 * side, 5 * side
            value = nn(tiles[halo_tile[(5 * e - 1, j, 3 * e)]], ext_s[3 * e, column])
            part_near[e, j] = (edge_near[e, side] + value).astype(bf16)
        x_near[e].start()

    far_order = [(i, j) for i in (-2, -1, 4, 5, 0, 1, 2, 3) for j in range(4)]
    count = sum(1 for i, j in jobs for _ in near_sources(i, j))
    rate = sum(1 for i, j in far_order for _ in zero_terms(i, j, False)) / count
    far, before, owed = zero_work(far_order), iter(()), 0.0
    for n, (i, j) in enumerate(jobs):
        here = pos[(i + 1) * 6 + j + 1]
        cols[n % 2, 0] = jnp.broadcast_to(here[0:1], (128, 256)).T
        cols[n % 2, 1] = jnp.broadcast_to(here[1:2], (128, 256)).T
        terms = []
        for q, (sr, column) in enumerate(near_sources(i, j)):
            if 1 <= column < 5:
                slot = 9 * (n % 2) + q
                terms.append((slot, sr, column))
            else:
                slot = 18 + len(halo_tile)
                halo_tile[(i, j, sr)] = slot
            make_tile(n % 2, slot, i, j, sr, column)
            owed += rate
            while owed >= 1.0:
                next(far, None)
                owed -= 1.0
            next(before, None)
        for _ in before:
            pass
        before = near_work(i, j, terms)
        if n == 4:
            recv_wait(ext_two.at[1 + py], 47 + py)
            recv_wait(ext_two.at[3 + py], 49 + py)
            x_two(2).start()
            x_two(3).start()
            x_zero[2].start()
            x_zero[3].start()
        if n == 11:
            recv_wait(ext_two.at[py], 46 + py)
            recv_wait(ext_two.at[4 + py], 50 + py)
            x_two(4).start()
            for c in x_one + x_zero[4:] + x_samples[2:]:
                c.start()
        if n in (13, 16):
            while next(far, False):
                owed -= 1.0
        if n == 13:
            level_two()
            for c in x_samples[:2]:
                c.wait()
            for e in range(2):

                @pl.when(px == e)
                def _():
                    near_edge(e)

        if n == 16:
            for c in x_zero[:4]:
                c.wait()
            for e in range(2):

                @pl.when(px == e)
                def _():
                    far_edge(e)

    for _ in before:
        pass
    for _ in far:
        pass

    c_loads[1].wait()
    for c in x_one:
        c.wait()

    def far_one_row(i):
        for j in range(2):
            total = None
            for sr in range(2):
                for b in range(6):
                    u, v = sr - i, b - 2 - j
                    if not far_pair(u, v):
                        continue
                    a = sr + 2 if 0 <= i < 2 else (sr + 4 if i < 0 else sr)
                    m = mask_one[i + 2, j, pl.ds(a * 8 + b, 1), :]
                    m = jnp.concatenate([m, m], axis=1).astype(bf16)
                    term = coupled(ext_one[sr, b] * m, coup, 1, u, v)
                    total = term if total is None else total + term
            if i < 0:
                part_one[0, i + 2, j] = total.astype(bf16)
            elif i > 1:
                part_one[1, i - 2, j] = total.astype(bf16)
            else:
                field_one[i, j] = total

    far_one_row(-2)
    far_one_row(-1)
    x_far.append(remote(part_one.at[0], got_one.at[1], 24, up))
    x_far[2].start()
    far_one_row(2)
    far_one_row(3)
    x_far.append(remote(part_one.at[1], got_one.at[0], 25, down))
    x_far[3].start()

    far_one_row(0)
    far_one_row(1)

    for c in x_zero[4:]:
        c.wait()
    for e in range(2):

        @pl.when(px != e)
        def _():
            far_edge(e)

    for i in range(4):
        halo_row(i)

    for k in range(6):

        @pl.when(k != 2 + px)
        def _():
            x_part_two(k).wait_send()
            recv_wait(got_two.at[k], 52 + k)

    got_two[2 + px] = part_two[2 + px]
    total = got_two[0].astype(f32)
    for k in range(1, 6):
        total += got_two[k].astype(f32)
    down_two = total.astype(bf16)
    for c in x_far[2:]:
        c.wait()
    down_one = []
    for i in range(2):
        for j in range(2):
            value = field_one[i, j] + nt(down_two, ttwo[i, j])
            value += got_one[0, i, j].astype(f32) + got_one[1, i, j].astype(f32)
            part_one[0, i, j] = value.astype(bf16)

    for c in x_far[:2]:
        c.wait()

    def descend(n, c):
        i, h = n // 2, lax.rem(n, 2)
        for b in range(2):
            j = 2 * h + b
            value = field_zero[i, j] + nt(part_one[0, i // 2, h], tone[i, j])
            down_zero[i, j] = (value + got_zero[i, j].astype(f32)).astype(bf16)
        return c

    lax.fori_loop(0, 8, descend, 0)

    for c in x_samples[2:]:
        c.wait()
    for e in range(2):

        @pl.when(px != e)
        def _():
            near_edge(e)

    def store(i):
        return pltpu.make_async_copy(part_zero.at[i], out.at[i], out_sem.at[i])

    for i in (1, 2, 0, 3):
        for j in range(4):
            value = near_sum[i, j] + nt(basis[i, j], down_zero[i, j])
            if j in (0, 3):
                for sr in range(max(i - 1, 0), min(i + 1, 3) + 1):
                    value += nn(tiles[halo_tile[(i, j, sr)]], ext_s[sr, 5 * (j // 3)])
            if i in (1, 2):
                part_zero[i, j] = value.astype(bf16)
            else:
                near_sum[i, j] = value
        if i in (1, 2):
            store(i).start()
    for c in x_near:
        c.wait()
    for e in range(2):
        for j in range(4):
            part_zero[3 * e, j] = (near_sum[3 * e, j] + got_near[e, j].astype(f32)).astype(bf16)
        store(3 * e).start()
    for i in range(4):
        store(i).wait()


def solution(mesh):
    nx, ny = mesh.shape["qx"], mesh.shape["qy"]

    def per_device(
        positions,
        samples,
        leaf_basis,
        transfer_one,
        transfer_two,
        couplings,
        near_lists,
        far_zero,
        far_one,
        far_two,
    ):
        def body(*refs):
            kernel(4 * nx, 4 * ny, *refs)

        hbm = pl.BlockSpec(memory_space=pl.ANY)
        vmem = pl.BlockSpec(memory_space=pltpu.VMEM)
        block = (256, 256)
        return pl.pallas_call(
            body,
            out_shape=jax.ShapeDtypeStruct(samples.shape, bf16),
            in_specs=[hbm] * 6 + [vmem] * 4,
            out_specs=hbm,
            scratch_shapes=[
                pltpu.VMEM((4, 4) + block, bf16),
                pltpu.VMEM((4, 4) + block, bf16),
                pltpu.VMEM((2, 2) + block, bf16),
                pltpu.VMEM((3, 20) + block, bf16),
                pltpu.VMEM((36, 2, 256), f32),
                pltpu.VMEM((4, 6) + block, bf16),
                pltpu.VMEM((4, 8) + block, bf16),
                pltpu.VMEM((2, 6) + block, bf16),
                pltpu.VMEM((6,) + block, bf16),
                pltpu.VMEM((4, 4) + block, f32),
                pltpu.VMEM((2, 2) + block, f32),
                pltpu.VMEM((4, 4) + block, f32),
                pltpu.VMEM((4, 4) + block, bf16),
                pltpu.VMEM((4, 4) + block, bf16),
                pltpu.VMEM((2, 2, 2) + block, bf16),
                pltpu.VMEM((2, 2, 2) + block, bf16),
                pltpu.VMEM((6,) + block, bf16),
                pltpu.VMEM((6,) + block, bf16),
                pltpu.VMEM((2, 4) + block, bf16),
                pltpu.VMEM((2, 4) + block, bf16),
                pltpu.VMEM((8, 4, 48, 128), f32),
                pltpu.VMEM((6, 2, 48, 128), f32),
                pltpu.VMEM((6, 8, 128), f32),
                pltpu.VMEM((48, 128), f32),
                pltpu.VMEM((6, 4, 24, 128), f32),
                pltpu.VMEM((42,) + block, bf16),
                pltpu.VMEM((2, 2, 256, 128), f32),
                pltpu.VMEM((4, 4) + block, f32),
                pltpu.VMEM((2, 2) + block, f32),
                pltpu.VMEM((4, 4) + block, bf16),
                pltpu.SemaphoreType.DMA((13,)),
                pltpu.SemaphoreType.DMA((36,)),
                pltpu.SemaphoreType.DMA((4,)),
                pltpu.SemaphoreType.DMA((58,)),
                pltpu.SemaphoreType.DMA((58,)),
            ],
            compiler_params=pltpu.CompilerParams(
                collective_id=0, has_side_effects=True, vmem_limit_bytes=60 << 20
            ),
        )(
            positions,
            samples,
            leaf_basis,
            transfer_one,
            transfer_two,
            couplings,
            near_lists,
            far_zero,
            far_one,
            far_two,
        )

    cell = P("qx", "qy", None, None)
    short = P("qx", "qy", None)
    return jax.shard_map(
        per_device,
        mesh=mesh,
        in_specs=(P(), cell, cell, cell, cell, P(), short, short, short, short),
        out_specs=cell,
        check_vma=False,
    )
```
